512 devices in a mesh: row: 32 (over z, core), col: 16 (over x, y).
Axes of the slice: x: 4, y: 4, z: 16, core: 2. Of those that a mesh axis runs over, the one named last changes fastest.
Arguments:
- records: float32 [9, 4096], P(None, 'row'), may hold values from -0.3 to 703, as said below
- pattern: int32 [32, 32], replicated, may hold values from 0 to 1, as said below
- iterate: float32 [4096, 4096], P('row', 'col'), may hold values from -0.5 to 0.5, as said below
Outputs:
- margin: float32 [4096, 4096], P('row', 'col')
- updated: float32 [4096, 4096], P('row', 'col')
The draws below stay inside these ranges and needn't reach their ends.
Inputs may be any that keep to these rules, and one draw needn't show every extreme that they name: `pattern`: symmetric 0 or 1 entries; the diagonal and the first off-diagonals are 1. `records`: exponents and coefficients are positive. `iterate`: symmetric.
All inputs are finite; a program needn't handle non-finite values.
Results may differ from the reference program's by a relative error of at most 0.0003.
Values sent between devices are 32-bit elements; how exact they have to be, the bound alone decides.
No kernel may reach another device: no remote copies, remote signals or barrier semaphores. Data moves between devices by JAX's collectives and lax.ppermute only.
A program may use at most 64 MiB of HBM per device.

```python
import math
import jax
import jax.numpy as jnp
from jax import lax

BLOCK = 128
PRIMS = 3
NB = 32
NFUN = 4096


def brick_layout(key):
    layout_key = jax.random.fold_in(key, 11)
    width_key, height_key = jax.random.split(layout_key)
    cube_side = int(math.pow(NB, 1.0 / 3.0) + 0.5)
    layer_width = jax.random.randint(width_key, (), 2, cube_side + 2)
    layer_height = 2 * jax.random.randint(height_key, (), max(1, cube_side // 2), cube_side // 2 + 2)
    positions = jnp.arange(NB, dtype=jnp.int32)
    layer_ids = positions // (layer_width * layer_height)
    within_layer = positions % (layer_width * layer_height)
    lane_row = within_layer // layer_width
    lane_pos = within_layer % layer_width
    brick_x = jnp.where(lane_row % 2 == 1, layer_width - 1 - lane_pos, lane_pos)
    brick_y = jnp.where(layer_ids % 2 == 1, layer_height - 1 - lane_row, lane_row)
    return (brick_x, brick_y, layer_ids)


def draw_records(key, part):
    brick_x, brick_y, brick_z = brick_layout(key)
    jitter_key, spread_key, weight_key = jax.random.split(jax.random.fold_in(key, 37), 3)
    function_ids = jnp.arange(NFUN, dtype=jnp.int32)
    block_ids = function_ids // BLOCK
    atom_slot = function_ids % BLOCK // 8
    lattice_x = 4 * brick_x[block_ids] + atom_slot % 4
    lattice_y = 2 * brick_y[block_ids] + atom_slot // 4 % 2
    lattice_z = 2 * brick_z[block_ids] + atom_slot // 8
    lattice = jnp.stack([lattice_x, lattice_y, lattice_z]).astype(jnp.float32)
    jitter = jnp.clip(0.12 * jax.random.normal(jitter_key, (3, NFUN // 8), jnp.float32), -0.3, 0.3)
    centers = 2.6 * lattice + jnp.repeat(jitter, 8, axis=1)
    shell_rank = (function_ids % 8).astype(jnp.float32)
    spread = jnp.exp(jax.random.uniform(spread_key, (NFUN,), jnp.float32, math.log(0.8), math.log(1.25)))
    outer = 0.1 * jnp.exp(shell_rank * math.log(2.4)) * spread
    factors = jnp.exp(jnp.arange(PRIMS).astype(jnp.float32) * math.log(3.5))
    exponents = factors[:, None] * outer[None, :]
    coefficients = jax.random.uniform(weight_key, (PRIMS, NFUN), jnp.float32, 0.2, 1.0)
    return jnp.concatenate([centers, exponents, coefficients], 0).astype(jnp.float32)


def draw_pattern(key, part):
    brick_x, brick_y, brick_z = brick_layout(key)
    gap_x = jnp.maximum(4 * jnp.abs(brick_x[:, None] - brick_x[None, :]) - 3, 0)
    gap_y = jnp.maximum(2 * jnp.abs(brick_y[:, None] - brick_y[None, :]) - 1, 0)
    gap_z = jnp.maximum(2 * jnp.abs(brick_z[:, None] - brick_z[None, :]) - 1, 0)
    near_blocks = gap_x * gap_x + gap_y * gap_y + gap_z * gap_z <= 2
    positions = jnp.arange(NB, dtype=jnp.int32)
    chain_near = jnp.abs(positions[:, None] - positions[None, :]) <= 1
    far_draws = jax.random.randint(jax.random.fold_in(key, 23), (NB, NB), 0, 20)
    listed = near_blocks | chain_near | (far_draws < 2)
    return (listed | listed.T).astype(jnp.int32)


def draw_iterate(key, part):
    noise = jnp.clip(jax.random.normal(key, (NFUN, NFUN), jnp.float32), -6.0, 6.0)
    symmetric = (noise + noise.T) * (0.15 / math.sqrt(2.0 * NFUN))
    positions = jnp.arange(NFUN)
    identity = (positions[:, None] == positions[None, :]).astype(jnp.float32)
    return (0.35 * identity + symmetric).astype(jnp.float32)


def setup_inputs(seed: int = 0) -> dict:
    key_list = jax.random.split(jax.random.key(seed), 4)
    return {
        "records": draw_records(jax.random.fold_in(key_list[3], 71), 0),
        "pattern": draw_pattern(jax.random.fold_in(key_list[3], 71), 0),
        "iterate": draw_iterate(jax.random.fold_in(key_list[3], 71), 0),
    }


def expand(blocks, size):
    row_blocks, col_blocks = blocks.shape
    grown = jnp.broadcast_to(blocks[:, None, :, None], (row_blocks, size, col_blocks, size))
    return grown.reshape(row_blocks * size, col_blocks * size).astype(jnp.float32)

def pair_margin(left, right):
    distance = (left[0][:, None] - right[0][None, :]) ** 2
    distance = distance + (left[1][:, None] - right[1][None, :]) ** 2
    distance = distance + (left[2][:, None] - right[2][None, :]) ** 2
    accumulated = jnp.zeros(distance.shape, jnp.float32)
    for p in range(PRIMS):
        for q in range(PRIMS):
            exponent_a = left[3 + p][:, None]
            exponent_b = right[3 + q][None, :]
            summed = exponent_a + exponent_b
            prefactor = (2.0 * jnp.sqrt(exponent_a * exponent_b) / summed) ** 1.5
            weight_ab = left[3 + PRIMS + p][:, None] * right[3 + PRIMS + q][None, :]
            accumulated = accumulated + weight_ab * prefactor * jnp.exp(-(exponent_a * exponent_b / summed) * distance)
    return accumulated

def self_norm(recs):
    accumulated = jnp.zeros(recs.shape[1], jnp.float32)
    for p in range(PRIMS):
        for q in range(PRIMS):
            exponent_a = recs[3 + p]
            exponent_b = recs[3 + q]
            prefactor = (2.0 * jnp.sqrt(exponent_a * exponent_b) / (exponent_a + exponent_b)) ** 1.5
            accumulated = accumulated + recs[3 + PRIMS + p] * recs[3 + PRIMS + q] * prefactor
    return accumulated

def matmul(left, right):
    return jnp.dot(left, right, precision=lax.Precision.HIGHEST, preferred_element_type=jnp.float32)

def reference(records, pattern, iterate):
    mask = expand(pattern, BLOCK)
    norms = self_norm(records)
    margin = mask * (pair_margin(records, records) / jnp.sqrt(norms[:, None] * norms[None, :]))
    masked = mask * iterate
    product_one = mask * matmul(margin, masked)
    product_two = mask * matmul(masked, product_one)
    product_three = matmul(product_two, masked)
    updated = mask * (1.5 * masked - 0.5 * product_three)
    return (margin, updated)
```

```python
import jax
import jax.numpy as jnp
from jax import lax
from jax.experimental import pallas as pl
from jax.experimental.pallas import tpu as pltpu
from jax.sharding import PartitionSpec as P

BLOCK = 128
PRIMS = 3
NB = 32
FIELDS = 3 + 3 * PRIMS
CHUNK = 32
VMEM = pltpu.VMEM
SMEM = pltpu.SMEM


def split(value):
    high = value.astype(jnp.bfloat16)
    low = (value - high.astype(jnp.float32)).astype(jnp.bfloat16)
    return high, low


def product(left, right, right_dim):
    left_high, left_low = split(left)
    right_high, right_low = split(right)
    dims = (((1,), (right_dim,)), ((), ()))

    def dot(a, b):
        return lax.dot_general(a, b, dims, preferred_element_type=jnp.float32)

    return dot(left_high, right_high) + (dot(left_high, right_low) + dot(left_low, right_high))


def half_tile(fields_ref, left_ref, tile_ref, half, block):
    right = [fields_ref[f, pl.ds(block, 1), :] for f in range(FIELDS)]

    def chunk(step, carry):
        rows = pl.ds(pl.multiple_of(step * CHUNK, CHUNK), CHUNK)
        left = [left_ref[half, f, rows, :] for f in range(FIELDS)]
        distance = (left[0] - right[0]) ** 2
        distance = distance + (left[1] - right[1]) ** 2
        distance = distance + (left[2] - right[2]) ** 2
        total = jnp.zeros_like(distance)
        for p in range(PRIMS):
            inner = jnp.zeros_like(distance)
            for q in range(PRIMS):
                inverse_root = lax.rsqrt(left[3 + p] + right[3 + q])
                root_rate = (left[6 + p] * inverse_root) * right[6 + q]
                ratio = jnp.maximum(root_rate * inverse_root, 1e-37)
                decay = jnp.exp(-(root_rate * root_rate) * distance)
                inner = inner + right[9 + q] * ((ratio * ratio * lax.rsqrt(ratio)) * decay)
            total = total + left[9 + p] * inner
        tile_ref[rows, :] = total
        return carry

    lax.fori_loop(0, BLOCK // CHUNK, chunk, 0)


def first_kernel(place, pattern, records, iterate_row, margin, product_one, fields, left, tile, acc):
    row, col = place[0], place[1]
    exponents = [records[:, 3 + p, :] for p in range(PRIMS)]
    coefficients = [records[:, 3 + PRIMS + p, :] for p in range(PRIMS)]
    roots = [jnp.sqrt(e) for e in exponents]
    norm = jnp.zeros_like(exponents[0])
    for p in range(PRIMS):
        for q in range(PRIMS):
            ratio = 2.0 * roots[p] * roots[q] / (exponents[p] + exponents[q])
            norm = norm + coefficients[p] * coefficients[q] * (ratio * jnp.sqrt(ratio))
    scale = (2.0**0.75) * lax.rsqrt(norm)
    for f in range(3):
        fields[f] = records[:, f, :]
    for p in range(PRIMS):
        fields[3 + p] = exponents[p]
        fields[6 + p] = roots[p]
        fields[9 + p] = coefficients[p] * scale
    for half in range(2):
        for f in range(FIELDS):
            own = jnp.broadcast_to(fields[f, pl.ds(2 * col + half, 1), :], (BLOCK, BLOCK))
            left[half, f] = own.T
        margin_live = pattern[row, 2 * col + half] != 0
        lanes = slice(half * BLOCK, (half + 1) * BLOCK)

        @pl.when(margin_live)
        def _():
            half_tile(fields, left, tile, half, row)
            margin[:, lanes] = tile[...].T

        @pl.when(jnp.logical_not(margin_live))
        def _():
            margin[:, lanes] = jnp.zeros((BLOCK, BLOCK), jnp.float32)

    acc[...] = jnp.zeros_like(acc)

    def step(index, carry):
        half, block = index // NB, index % NB
        own = 2 * col + half
        live = pattern[own, block] * pattern[block, row] * pattern[row, own]

        @pl.when(live != 0)
        def _():
            half_tile(fields, left, tile, half, block)
            lanes = pl.ds(pl.multiple_of((block % 2) * BLOCK, BLOCK), BLOCK)
            acc[half] += product(iterate_row[block // 2, :, lanes], tile[...], 1)

        return carry

    lax.fori_loop(0, 2 * NB, step, 0)
    product_one[:, :BLOCK] = acc[0]
    product_one[:, BLOCK:] = acc[1]


def second_kernel(place, pattern, one_row, iterate_col, slices, acc):
    row, col = place[0], place[1]
    acc[...] = jnp.zeros_like(acc)

    def step(index, carry):
        half, block = index // NB, index % NB
        own = 2 * col + half
        live = pattern[row, block] * pattern[block, own] * pattern[row, own]

        @pl.when(live != 0)
        def _():
            lanes = pl.ds(pl.multiple_of((block % 2) * BLOCK, BLOCK), BLOCK)
            rows = pl.ds(pl.multiple_of(block * BLOCK, BLOCK), BLOCK)
            own_lanes = pl.ds(pl.multiple_of(half * BLOCK, BLOCK), BLOCK)
            acc[half] += product(one_row[block // 2, :, lanes], iterate_col[rows, own_lanes], 0)

        return carry

    lax.fori_loop(0, 2 * NB, step, 0)
    for half in range(2):
        slices[:, half] = acc[half].T.reshape(BLOCK // 8, 8, BLOCK)


def third_kernel(place, pattern, two_row, iterate_col, iterate, updated, acc):
    row, col = place[0], place[1]
    acc[...] = jnp.zeros_like(acc)

    def step(index, carry):
        half, block = index // NB, index % NB
        own = 2 * col + half
        live = pattern[row, block] * pattern[block, own] * pattern[row, own]

        @pl.when(live != 0)
        def _():
            rows = pl.ds(pl.multiple_of(block * BLOCK, BLOCK), BLOCK)
            own_lanes = pl.ds(pl.multiple_of(half * BLOCK, BLOCK), BLOCK)
            piece = two_row[:, block].reshape(BLOCK, BLOCK)
            acc[half] += product(piece, iterate_col[rows, own_lanes], 0)

        return carry

    lax.fori_loop(0, 2 * NB, step, 0)
    for half in range(2):
        lanes = slice(half * BLOCK, (half + 1) * BLOCK)
        mask = (pattern[row, 2 * col + half] != 0).astype(jnp.float32)
        updated[:, lanes] = mask * (1.5 * iterate[:, lanes] - 0.5 * acc[half])


def spread(value, axis, count):
    return lax.all_to_all(jnp.broadcast_to(value[None], (count,) + value.shape), axis, 0, 0, tiled=True)


def call(kernel, out_shapes, scratch, *operands):
    whole = pl.BlockSpec(memory_space=VMEM)
    scalars = pl.BlockSpec(memory_space=SMEM)
    return pl.pallas_call(
        kernel,
        out_shape=out_shapes,
        in_specs=[scalars, scalars] + [whole] * (len(operands) - 2),
        out_specs=jax.tree.map(lambda _: whole, out_shapes),
        scratch_shapes=scratch,
    )(*operands)


def body(records, pattern, iterate):
    place = jnp.stack([lax.axis_index("row"), lax.axis_index("col")]).astype(jnp.int32)
    tile = jax.ShapeDtypeStruct((BLOCK, 2 * BLOCK), jnp.float32)
    acc = VMEM((2, BLOCK, BLOCK), jnp.float32)
    iterate_col = lax.all_gather(iterate, "row", axis=0, tiled=True)
    everyone = spread(records, "row", 32)
    iterate_row = spread(iterate, "col", 16)
    margin, product_one = call(
        first_kernel,
        (tile, tile),
        [
            VMEM((FIELDS, NB, BLOCK), jnp.float32),
            VMEM((2, FIELDS, BLOCK, BLOCK), jnp.float32),
            VMEM((BLOCK, BLOCK), jnp.float32),
            acc,
        ],
        place,
        pattern,
        everyone,
        iterate_row,
    )
    one_row = spread(product_one, "col", 16)
    slices = call(
        second_kernel,
        jax.ShapeDtypeStruct((16, 2, 8, BLOCK), jnp.float32),
        [acc],
        place,
        pattern,
        one_row,
        iterate_col,
    )
    slices = lax.all_to_all(slices, "col", 0, 0, tiled=True).reshape(NB, 8, BLOCK)
    slices = lax.all_to_all(slices, "row", 0, 0, tiled=True)
    two_row = spread(slices, "col", 16)
    updated = call(third_kernel, tile, [acc], place, pattern, two_row, iterate_col, iterate)
    return (margin, updated)


def solution(mesh):
    in_specs = (P(None, "row"), P(), P("row", "col"))
    out_specs = (P("row", "col"), P("row", "col"))
    return jax.shard_map(body, mesh=mesh, in_specs=in_specs, out_specs=out_specs, check_vma=False)
```

```python
import jax
import jax.numpy as jnp
from jax import lax
from jax.experimental import pallas as pl
from jax.experimental.pallas import tpu as pltpu
from jax.sharding import PartitionSpec as P


BLOCK = 128
PRIMS = 3
NB = 32
FIELDS = 3 + 3 * PRIMS
CHUNK = 32
LOG2E = 1.4426950408889634
VMEM = pltpu.VMEM
SMEM = pltpu.SMEM


def split(value):
    high = value.astype(jnp.bfloat16)
    low = (value - high.astype(jnp.float32)).astype(jnp.bfloat16)
    return high, low


def product(left, right, right_dim):
    left_high, left_low = split(left)
    right_high, right_low = split(right)
    dims = (((1,), (right_dim,)), ((), ()))

    def dot(a, b):
        return lax.dot_general(a, b, dims, preferred_element_type=jnp.float32)

    return dot(left_high, right_high) + (dot(left_high, right_low) + dot(left_low, right_high))


def half_tile(fields_ref, left_ref, tile_ref, half, block):
    right = [fields_ref[f, pl.ds(block, 1), :] for f in range(FIELDS)]

    def chunk(step, carry):
        rows = pl.ds(pl.multiple_of(step * CHUNK, CHUNK), CHUNK)
        left = [left_ref[half, f, rows, :] for f in range(FIELDS)]
        distance = (left[0] - right[0]) ** 2
        distance = distance + (left[1] - right[1]) ** 2
        distance = (distance + (left[2] - right[2]) ** 2) * -LOG2E
        total = jnp.zeros_like(distance)
        for p in range(PRIMS):
            inner = jnp.zeros_like(distance)
            for q in range(PRIMS):
                summed = left[3 + p] + right[3 + q]
                root = (left[6 + p] * lax.rsqrt(summed)) * right[6 + q]
                ratio = root * root
                decay = jnp.exp2(((ratio * summed) * ratio) * distance)
                inner = inner + right[9 + q] * ((ratio * root) * decay)
            total = total + left[9 + p] * inner
        tile_ref[rows, :] = total
        return carry

    lax.fori_loop(0, BLOCK // CHUNK, chunk, 0)


def spread_own(fields, left, col):
    for half in range(2):
        for f in range(FIELDS):
            own = jnp.broadcast_to(fields[f, pl.ds(2 * col + half, 1), :], (BLOCK, BLOCK))
            left[half, f] = own.T


def margin_kernel(place, pattern, records, fields, margin, left, tile):
    row, col = place[0], place[1]
    exponents = [records[:, 3 + p, :] for p in range(PRIMS)]
    coefficients = [records[:, 3 + PRIMS + p, :] for p in range(PRIMS)]
    roots = [jnp.sqrt(e) for e in exponents]
    norm = jnp.zeros_like(exponents[0])
    for p in range(PRIMS):
        for q in range(PRIMS):
            ratio = 2.0 * roots[p] * roots[q] / (exponents[p] + exponents[q])
            norm = norm + coefficients[p] * coefficients[q] * (ratio * jnp.sqrt(ratio))
    scale = (2.0**0.75) * lax.rsqrt(norm)
    for f in range(3):
        fields[f] = records[:, f, :]
    for p in range(PRIMS):
        fields[3 + p] = exponents[p]
        fields[6 + p] = jnp.sqrt(roots[p])
        fields[9 + p] = coefficients[p] * scale
    spread_own(fields, left, col)
    for half in range(2):
        margin_live = pattern[row, 2 * col + half] != 0
        lanes = slice(half * BLOCK, (half + 1) * BLOCK)

        @pl.when(margin_live)
        def _():
            half_tile(fields, left, tile, half, row)
            margin[:, lanes] = tile[...].T

        @pl.when(jnp.logical_not(margin_live))
        def _():
            margin[:, lanes] = jnp.zeros((BLOCK, BLOCK), jnp.float32)


def first_kernel(place, pattern, fields, iterate_row, product_one, left, tile, acc):
    row, col = place[0], place[1]
    spread_own(fields, left, col)
    acc[...] = jnp.zeros_like(acc)

    def step(index, carry):
        half, block = index // NB, index % NB
        own = 2 * col + half
        needed = pattern[own, block] * pattern[block, row] * pattern[row, own]

        @pl.when(needed != 0)
        def _():
            half_tile(fields, left, tile, half, block)
            lanes = pl.ds(pl.multiple_of((block % 2) * BLOCK, BLOCK), BLOCK)
            acc[half] += product(iterate_row[block // 2, :, lanes], tile[...], 1)

        return carry

    lax.fori_loop(0, 2 * NB, step, 0)
    product_one[:, :BLOCK] = acc[0]
    product_one[:, BLOCK:] = acc[1]


def prepare_kernel(place, pattern, iterate_col, high, low):
    col = place[1]

    def step(block, carry):
        rows = pl.ds(pl.multiple_of(block * BLOCK, BLOCK), BLOCK)
        for half in range(2):
            lanes = slice(half * BLOCK, (half + 1) * BLOCK)
            mask = (pattern[block, 2 * col + half] != 0).astype(jnp.float32)
            high[rows, lanes], low[rows, lanes] = split(mask * iterate_col[rows, lanes])
        return carry

    lax.fori_loop(0, NB, step, 0)


def contract(pieces, high, low):
    total = jnp.zeros((BLOCK, 2 * BLOCK), jnp.float32)
    for k, piece in enumerate(pieces):
        rows = slice(2 * BLOCK * k, 2 * BLOCK * (k + 1))
        piece_high, piece_low = split(piece)
        total = total + jnp.dot(piece_high, high[rows], preferred_element_type=jnp.float32)
        total = total + jnp.dot(piece_high, low[rows], preferred_element_type=jnp.float32)
        total = total + jnp.dot(piece_low, high[rows], preferred_element_type=jnp.float32)
    return total


def live(pattern, row, column):
    return (pattern[row, column] != 0).astype(jnp.float32)


def second_kernel(place, pattern, one_row, high, low, slices):
    row, col = place[0], place[1]
    total = contract([one_row[k] for k in range(16)], high, low)
    for half in range(2):
        own = total[:, half * BLOCK : (half + 1) * BLOCK]
        own = (live(pattern, row, 2 * col + half) * own).T
        slices[:, half] = own.reshape(BLOCK // 8, 8, BLOCK)


def third_kernel(place, pattern, two_row, high, low, iterate, updated):
    row, col = place[0], place[1]
    pieces = []
    for k in range(16):
        pair = [two_row[:, 2 * k + h].reshape(BLOCK, BLOCK) for h in range(2)]
        pieces.append(jnp.concatenate(pair, axis=1))
    total = contract(pieces, high, low)
    for half in range(2):
        lanes = slice(half * BLOCK, (half + 1) * BLOCK)
        mask = live(pattern, row, 2 * col + half)
        updated[:, lanes] = mask * (1.5 * iterate[:, lanes] - 0.5 * total[:, lanes])


def spread(value, axis, count):
    return lax.all_to_all(jnp.broadcast_to(value[None], (count,) + value.shape), axis, 0, 0, tiled=True)


def call(kernel, out_shapes, scratch, *operands):
    whole = pl.BlockSpec(memory_space=VMEM)
    scalars = pl.BlockSpec(memory_space=SMEM)
    return pl.pallas_call(
        kernel,
        out_shape=out_shapes,
        in_specs=[scalars, scalars] + [whole] * (len(operands) - 2),
        out_specs=jax.tree.map(lambda _: whole, out_shapes),
        scratch_shapes=scratch,
    )(*operands)


def stages(records, pattern, iterate):
    place = jnp.stack([lax.axis_index("row"), lax.axis_index("col")]).astype(jnp.int32)
    tile = jax.ShapeDtypeStruct((BLOCK, 2 * BLOCK), jnp.float32)
    panel = jax.ShapeDtypeStruct((NB * BLOCK, 2 * BLOCK), jnp.bfloat16)
    iterate_col = lax.all_gather(iterate, "row", axis=0, tiled=True)
    everyone = lax.all_gather(records, "row", axis=0)
    iterate_row = spread(iterate, "col", 16)
    left = VMEM((2, FIELDS, BLOCK, BLOCK), jnp.float32)
    square = VMEM((BLOCK, BLOCK), jnp.float32)
    acc = VMEM((2, BLOCK, BLOCK), jnp.float32)
    table = jax.ShapeDtypeStruct((FIELDS, NB, BLOCK), jnp.float32)
    fields, margin = call(margin_kernel, (table, tile), [left, square], place, pattern, everyone)
    product_one = call(first_kernel, tile, [left, square, acc], place, pattern, fields, iterate_row)
    one_row = spread(product_one, "col", 16)
    high, low = call(prepare_kernel, (panel, panel), [], place, pattern, iterate_col)
    slices = jax.ShapeDtypeStruct((16, 2, 8, BLOCK), jnp.float32)
    slices = call(second_kernel, slices, [], place, pattern, one_row, high, low)
    slices = lax.all_to_all(slices, "col", 0, 0, tiled=True).reshape(NB, 8, BLOCK)
    slices = lax.all_to_all(slices, "row", 0, 0, tiled=True)
    two_row = spread(slices, "col", 16)
    updated = call(third_kernel, tile, [], place, pattern, two_row, high, low, iterate)
    return (margin, updated)


def solution(mesh):
    in_specs = (P(None, "row"), P(), P("row", "col"))
    out_specs = (P("row", "col"), P("row", "col"))
    return jax.shard_map(stages, mesh=mesh, in_specs=in_specs, out_specs=out_specs, check_vma=False)
```

```python
import jax
import jax.numpy as jnp
from jax import lax
from jax.experimental import pallas as pl
from jax.experimental.pallas import tpu as pltpu
from jax.sharding import PartitionSpec as P


BLOCK = 128
PRIMS = 3
NB = 32
FIELDS = 3 + 3 * PRIMS
CHUNK = 32
LOG2E = 1.4426950408889634
VMEM = pltpu.VMEM
SMEM = pltpu.SMEM


def split(value):
    high = value.astype(jnp.bfloat16)
    low = (value - high.astype(jnp.float32)).astype(jnp.bfloat16)
    return high, low


def product(left, right, right_dim):
    left_high, left_low = split(left)
    right_high, right_low = split(right)
    dims = (((1,), (right_dim,)), ((), ()))

    def dot(a, b):
        return lax.dot_general(a, b, dims, preferred_element_type=jnp.float32)

    return dot(left_high, right_high) + (dot(left_high, right_low) + dot(left_low, right_high))


def half_tile(fields_ref, left_ref, tile_ref, half, block):
    right = [fields_ref[f, pl.ds(block, 1), :] for f in range(FIELDS)]

    def chunk(step, carry):
        rows = pl.ds(pl.multiple_of(step * CHUNK, CHUNK), CHUNK)
        left = [left_ref[half, f, rows, :] for f in range(FIELDS)]
        distance = (left[0] - right[0]) ** 2
        distance = distance + (left[1] - right[1]) ** 2
        distance = (distance + (left[2] - right[2]) ** 2) * -LOG2E
        total = jnp.zeros_like(distance)
        for p in range(PRIMS):
            inner = jnp.zeros_like(distance)
            for q in range(PRIMS):
                summed = left[3 + p] + right[3 + q]
                root = (left[6 + p] * lax.rsqrt(summed)) * right[6 + q]
                ratio = root * root
                decay = jnp.exp2(((ratio * summed) * ratio) * distance)
                inner = inner + right[9 + q] * ((ratio * root) * decay)
            total = total + left[9 + p] * inner
        tile_ref[rows, :] = total
        return carry

    lax.fori_loop(0, BLOCK // CHUNK, chunk, 0)


def spread_own(fields, left, col):
    for half in range(2):
        for f in range(FIELDS):
            own = jnp.broadcast_to(fields[f, pl.ds(2 * col + half, 1), :], (BLOCK, BLOCK))
            left[half, f] = own.T


def margin_kernel(place, pattern, records, fields, margin, left, tile):
    row, col = place[0], place[1]
    exponents = [records[:, 3 + p, :] for p in range(PRIMS)]
    coefficients = [records[:, 3 + PRIMS + p, :] for p in range(PRIMS)]
    roots = [jnp.sqrt(e) for e in exponents]
    norm = jnp.zeros_like(exponents[0])
    for p in range(PRIMS):
        for q in range(PRIMS):
            ratio = 2.0 * roots[p] * roots[q] / (exponents[p] + exponents[q])
            norm = norm + coefficients[p] * coefficients[q] * (ratio * jnp.sqrt(ratio))
    scale = (2.0**0.75) * lax.rsqrt(norm)
    for f in range(3):
        fields[f] = records[:, f, :]
    for p in range(PRIMS):
        fields[3 + p] = exponents[p]
        fields[6 + p] = jnp.sqrt(roots[p])
        fields[9 + p] = coefficients[p] * scale
    spread_own(fields, left, col)
    for half in range(2):
        margin_live = pattern[row, 2 * col + half] != 0
        lanes = slice(half * BLOCK, (half + 1) * BLOCK)

        @pl.when(margin_live)
        def _():
            half_tile(fields, left, tile, half, row)
            margin[:, lanes] = tile[...].T

        @pl.when(jnp.logical_not(margin_live))
        def _():
            margin[:, lanes] = jnp.zeros((BLOCK, BLOCK), jnp.float32)


def first_kernel(place, pattern, fields, iterate_row, product_one, left, tile, acc):
    row, col = place[0], place[1]
    spread_own(fields, left, col)
    acc[...] = jnp.zeros_like(acc)

    def step(index, carry):
        half, block = index // NB, index % NB
        own = 2 * col + half
        needed = pattern[own, block] * pattern[block, row] * pattern[row, own]

        @pl.when(needed != 0)
        def _():
            half_tile(fields, left, tile, half, block)
            lanes = pl.ds(pl.multiple_of((block % 2) * BLOCK, BLOCK), BLOCK)
            acc[half] += product(iterate_row[block // 2, :, lanes], tile[...], 1)

        return carry

    lax.fori_loop(0, 2 * NB, step, 0)
    for copy in range(16):
        product_one[copy, :, :BLOCK] = acc[0]
        product_one[copy, :, BLOCK:] = acc[1]


def replicate_kernel(place, pattern, value, copies):
    for copy in range(copies.shape[0]):
        copies[copy] = value[...]


def prepare_kernel(place, pattern, iterate_col, high, low):
    col = place[1]

    def step(block, carry):
        rows = pl.ds(pl.multiple_of(block * BLOCK, BLOCK), BLOCK)
        for half in range(2):
            lanes = slice(half * BLOCK, (half + 1) * BLOCK)
            mask = (pattern[block, 2 * col + half] != 0).astype(jnp.float32)
            high[rows, lanes], low[rows, lanes] = split(mask * iterate_col[rows, lanes])
        return carry

    lax.fori_loop(0, NB, step, 0)


def contract(pieces, high, low):
    total = jnp.zeros((BLOCK, 2 * BLOCK), jnp.float32)
    for k, piece in enumerate(pieces):
        rows = slice(2 * BLOCK * k, 2 * BLOCK * (k + 1))
        piece_high, piece_low = split(piece)
        total = total + jnp.dot(piece_high, high[rows], preferred_element_type=jnp.float32)
        total = total + jnp.dot(piece_high, low[rows], preferred_element_type=jnp.float32)
        total = total + jnp.dot(piece_low, high[rows], preferred_element_type=jnp.float32)
    return total


def live(pattern, row, column):
    return (pattern[row, column] != 0).astype(jnp.float32)


def second_kernel(place, pattern, one_row, high, low, slices):
    row, col = place[0], place[1]
    total = contract([one_row[k] for k in range(16)], high, low)
    for half in range(2):
        own = total[:, half * BLOCK : (half + 1) * BLOCK]
        own = (live(pattern, row, 2 * col + half) * own).T
        slices[:, half] = own.reshape(BLOCK // 8, 8, BLOCK)


def third_kernel(place, pattern, two_row, high, low, iterate, updated):
    row, col = place[0], place[1]
    pieces = []
    for k in range(16):
        pair = [two_row[:, 2 * k + h].reshape(BLOCK, BLOCK) for h in range(2)]
        pieces.append(jnp.concatenate(pair, axis=1))
    total = contract(pieces, high, low)
    for half in range(2):
        lanes = slice(half * BLOCK, (half + 1) * BLOCK)
        mask = live(pattern, row, 2 * col + half)
        updated[:, lanes] = mask * (1.5 * iterate[:, lanes] - 0.5 * total[:, lanes])


def exchange(pieces, axis):
    return lax.all_to_all(pieces, axis, 0, 0, tiled=True)


def call(kernel, out_shapes, scratch, *operands, on_chip=()):
    whole = pl.BlockSpec(memory_space=VMEM)
    scalars = pl.BlockSpec(memory_space=SMEM)
    operands = list(operands)
    for k in on_chip:
        operands[k] = pltpu.with_memory_space_constraint(operands[k], VMEM)
    return pl.pallas_call(
        kernel,
        out_shape=out_shapes,
        in_specs=[scalars, scalars] + [whole] * (len(operands) - 2),
        out_specs=jax.tree.map(lambda _: whole, out_shapes),
        scratch_shapes=scratch,
        compiler_params=pltpu.CompilerParams(vmem_limit_bytes=24 * 2**20),
    )(*operands)


def stages(records, pattern, iterate):
    place = jnp.stack([lax.axis_index("row"), lax.axis_index("col")]).astype(jnp.int32)
    tile = jax.ShapeDtypeStruct((BLOCK, 2 * BLOCK), jnp.float32)
    panel = VMEM((NB * BLOCK, 2 * BLOCK), jnp.bfloat16)
    tiles = jax.ShapeDtypeStruct((16, BLOCK, 2 * BLOCK), jnp.float32)
    iterate_col = lax.all_gather(iterate, "row", axis=0, tiled=True)
    everyone = lax.all_gather(records, "row", axis=0)
    iterate_row = exchange(jnp.broadcast_to(iterate[None], tiles.shape), "col")
    left = VMEM((2, FIELDS, BLOCK, BLOCK), jnp.float32)
    square = VMEM((BLOCK, BLOCK), jnp.float32)
    acc = VMEM((2, BLOCK, BLOCK), jnp.float32)
    table = jax.ShapeDtypeStruct((FIELDS, NB, BLOCK), jnp.float32)
    fields, margin = call(margin_kernel, (table, tile), [left, square], place, pattern, everyone)
    product_one = call(
        first_kernel, tiles, [left, square, acc], place, pattern, fields, iterate_row, on_chip=(3,)
    )
    one_row = exchange(product_one, "col")
    high, low = call(prepare_kernel, (panel, panel), [], place, pattern, iterate_col)
    slices = VMEM((16, 2, 8, BLOCK), jnp.float32)
    slices = call(second_kernel, slices, [], place, pattern, one_row, high, low, on_chip=(2, 3, 4))
    slices = exchange(slices, "col").reshape(NB, 8, BLOCK)
    slices = exchange(slices, "row")
    slices = call(
        replicate_kernel, VMEM((16, NB, 8, BLOCK), jnp.float32), [], place, pattern, slices, on_chip=(2,)
    )
    two_row = exchange(slices, "col")
    updated = call(third_kernel, tile, [], place, pattern, two_row, high, low, iterate, on_chip=(2, 3, 4))
    return (margin, updated)


def solution(mesh):
    in_specs = (P(None, "row"), P(), P("row", "col"))
    out_specs = (P("row", "col"), P("row", "col"))
    return jax.shard_map(stages, mesh=mesh, in_specs=in_specs, out_specs=out_specs, check_vma=False)
```

```python
import jax
import jax.numpy as jnp
from jax import lax
from jax.experimental import pallas as pl
from jax.experimental.pallas import tpu as pltpu
from jax.sharding import PartitionSpec as P


BLOCK = 128
PRIMS = 3
NB = 32
FIELDS = 3 + 3 * PRIMS
CHUNK = 32
LOG2E = 1.4426950408889634
VMEM = pltpu.VMEM
SMEM = pltpu.SMEM


def split(value):
    high = value.astype(jnp.bfloat16)
    low = (value - high.astype(jnp.float32)).astype(jnp.bfloat16)
    return high, low


def product(left, right, right_dim):
    left_high, left_low = split(left)
    right_high, right_low = split(right)
    dims = (((1,), (right_dim,)), ((), ()))

    def dot(a, b):
        return lax.dot_general(a, b, dims, preferred_element_type=jnp.float32)

    return dot(left_high, right_high) + (dot(left_high, right_low) + dot(left_low, right_high))


def half_tile(fields_ref, left_ref, tile_ref, half, block):
    right = [fields_ref[f, pl.ds(block, 1), :] for f in range(FIELDS)]

    def chunk(step, carry):
        rows = pl.ds(pl.multiple_of(step * CHUNK, CHUNK), CHUNK)
        left = [left_ref[half, f, rows, :] for f in range(FIELDS)]
        distance = (left[0] - right[0]) ** 2
        distance = distance + (left[1] - right[1]) ** 2
        distance = (distance + (left[2] - right[2]) ** 2) * -LOG2E
        total = jnp.zeros_like(distance)
        for p in range(PRIMS):
            inner = jnp.zeros_like(distance)
            for q in range(PRIMS):
                summed = left[3 + p] + right[3 + q]
                root = (left[6 + p] * lax.rsqrt(summed)) * right[6 + q]
                ratio = root * root
                decay = jnp.exp2(((ratio * summed) * ratio) * distance)
                inner = inner + right[9 + q] * ((ratio * root) * decay)
            total = total + left[9 + p] * inner
        tile_ref[rows, :] = total
        return carry

    lax.fori_loop(0, BLOCK // CHUNK, chunk, 0)


def spread_own(fields, left, col):
    for half in range(2):
        for f in range(FIELDS):
            own = jnp.broadcast_to(fields[f, pl.ds(2 * col + half, 1), :], (BLOCK, BLOCK))
            left[half, f] = own.T


def margin_kernel(place, pattern, records, fields, margin, left, tile):
    row, col = place[0], place[1]
    exponents = [records[:, 3 + p, :] for p in range(PRIMS)]
    coefficients = [records[:, 3 + PRIMS + p, :] for p in range(PRIMS)]
    roots = [jnp.sqrt(e) for e in exponents]
    norm = jnp.zeros_like(exponents[0])
    for p in range(PRIMS):
        for q in range(PRIMS):
            ratio = 2.0 * roots[p] * roots[q] / (exponents[p] + exponents[q])
            norm = norm + coefficients[p] * coefficients[q] * (ratio * jnp.sqrt(ratio))
    scale = (2.0**0.75) * lax.rsqrt(norm)
    for f in range(3):
        fields[f] = records[:, f, :]
    for p in range(PRIMS):
        fields[3 + p] = exponents[p]
        fields[6 + p] = jnp.sqrt(roots[p])
        fields[9 + p] = coefficients[p] * scale
    spread_own(fields, left, col)
    for half in range(2):
        margin_live = pattern[row, 2 * col + half] != 0
        lanes = slice(half * BLOCK, (half + 1) * BLOCK)

        @pl.when(margin_live)
        def _():
            half_tile(fields, left, tile, half, row)
            margin[:, lanes] = tile[...].T

        @pl.when(jnp.logical_not(margin_live))
        def _():
            margin[:, lanes] = jnp.zeros((BLOCK, BLOCK), jnp.float32)


def first_kernel(place, pattern, fields, iterate_row, product_one, left, tile, acc):
    row, col = place[0], place[1]
    spread_own(fields, left, col)
    acc[...] = jnp.zeros_like(acc)

    def step(index, carry):
        half, block = index // NB, index % NB
        own = 2 * col + half
        needed = pattern[own, block] * pattern[block, row] * pattern[row, own]

        @pl.when(needed != 0)
        def _():
            half_tile(fields, left, tile, half, block)
            lanes = pl.ds(pl.multiple_of((block % 2) * BLOCK, BLOCK), BLOCK)
            acc[half] += product(iterate_row[block // 2, :, lanes], tile[...], 1)

        return carry

    lax.fori_loop(0, 2 * NB, step, 0)
    for copy in range(16):
        product_one[copy, :, :BLOCK] = acc[0]
        product_one[copy, :, BLOCK:] = acc[1]


def replicate_kernel(place, pattern, value, copies):
    for copy in range(copies.shape[0]):
        copies[copy] = value[...]


def prepare_kernel(place, pattern, iterate_col, high, low):
    col = place[1]

    def step(block, carry):
        rows = pl.ds(pl.multiple_of(block * BLOCK, BLOCK), BLOCK)
        for half in range(2):
            lanes = slice(half * BLOCK, (half + 1) * BLOCK)
            mask = (pattern[block, 2 * col + half] != 0).astype(jnp.float32)
            high[rows, lanes], low[rows, lanes] = split(mask * iterate_col[rows, lanes])
        return carry

    lax.fori_loop(0, NB, step, 0)


def contract(pieces, high, low):
    total = jnp.zeros((BLOCK, 2 * BLOCK), jnp.float32)
    for k, piece in enumerate(pieces):
        rows = slice(2 * BLOCK * k, 2 * BLOCK * (k + 1))
        piece_high, piece_low = split(piece)
        total = total + jnp.dot(piece_high, high[rows], preferred_element_type=jnp.float32)
        total = total + jnp.dot(piece_high, low[rows], preferred_element_type=jnp.float32)
        total = total + jnp.dot(piece_low, high[rows], preferred_element_type=jnp.float32)
    return total


def live(pattern, row, column):
    return (pattern[row, column] != 0).astype(jnp.float32)


def second_kernel(place, pattern, one_row, high, low, kept, given, tile):
    row, col = place[0], place[1]
    total = contract([one_row[k] for k in range(16)], high, low)
    for half in range(2):
        own = total[:, half * BLOCK : (half + 1) * BLOCK]
        tile[half] = (live(pattern, row, 2 * col + half) * own).T
    core = row % 2
    kept[...] = tile[core].reshape(BLOCK // 8, 8, BLOCK)
    given[...] = tile[1 - core].reshape(BLOCK // 8, 8, BLOCK)


def third_kernel(place, pattern, two_row, high, low, iterate, updated):
    row, col = place[0], place[1]
    core = row % 2
    pieces = []
    for k in range(16):
        pair = [two_row[:, k, core ^ h].reshape(BLOCK, BLOCK) for h in range(2)]
        pieces.append(jnp.concatenate(pair, axis=1))
    total = contract(pieces, high, low)
    for half in range(2):
        lanes = slice(half * BLOCK, (half + 1) * BLOCK)
        mask = live(pattern, row, 2 * col + half)
        updated[:, lanes] = mask * (1.5 * iterate[:, lanes] - 0.5 * total[:, lanes])


def exchange(pieces, axis):
    return lax.all_to_all(pieces, axis, 0, 0, tiled=True)


def call(kernel, out_shapes, scratch, *operands, on_chip=()):
    whole = pl.BlockSpec(memory_space=VMEM)
    scalars = pl.BlockSpec(memory_space=SMEM)
    operands = list(operands)
    for k in on_chip:
        operands[k] = pltpu.with_memory_space_constraint(operands[k], VMEM)
    return pl.pallas_call(
        kernel,
        out_shape=out_shapes,
        in_specs=[scalars, scalars] + [whole] * (len(operands) - 2),
        out_specs=jax.tree.map(lambda _: whole, out_shapes),
        scratch_shapes=scratch,
        compiler_params=pltpu.CompilerParams(vmem_limit_bytes=24 * 2**20),
    )(*operands)


def stages(records, pattern, iterate):
    place = jnp.stack([lax.axis_index("row"), lax.axis_index("col")]).astype(jnp.int32)
    tile = jax.ShapeDtypeStruct((BLOCK, 2 * BLOCK), jnp.float32)
    panel = VMEM((NB * BLOCK, 2 * BLOCK), jnp.bfloat16)
    tiles = jax.ShapeDtypeStruct((16, BLOCK, 2 * BLOCK), jnp.float32)
    iterate_col = lax.all_gather(iterate, "row", axis=0, tiled=True)
    everyone = lax.all_gather(records, "row", axis=0)
    iterate_row = exchange(jnp.broadcast_to(iterate[None], tiles.shape), "col")
    left = VMEM((2, FIELDS, BLOCK, BLOCK), jnp.float32)
    square = VMEM((BLOCK, BLOCK), jnp.float32)
    acc = VMEM((2, BLOCK, BLOCK), jnp.float32)
    table = jax.ShapeDtypeStruct((FIELDS, NB, BLOCK), jnp.float32)
    fields, margin = call(margin_kernel, (table, tile), [left, square], place, pattern, everyone)
    product_one = call(
        first_kernel, tiles, [left, square, acc], place, pattern, fields, iterate_row, on_chip=(3,)
    )
    one_row = exchange(product_one, "col")
    high, low = call(prepare_kernel, (panel, panel), [], place, pattern, iterate_col)
    half = VMEM((16, 8, BLOCK), jnp.float32)
    turned = VMEM((2, BLOCK, BLOCK), jnp.float32)
    kept, given = call(
        second_kernel, (half, half), [turned], place, pattern, one_row, high, low, on_chip=(2, 3, 4)
    )
    given = lax.ppermute(given, "row", [(r, r ^ 1) for r in range(NB)])
    slices = jnp.stack([kept, given], axis=1)
    slices = exchange(slices, "col")
    cores = [[2 * z + core for z in range(16)] for core in range(2)]
    slices = lax.all_to_all(slices, "row", 0, 0, tiled=True, axis_index_groups=cores)
    copies = VMEM((16,) + slices.shape, jnp.float32)
    slices = call(replicate_kernel, copies, [], place, pattern, slices, on_chip=(2,))
    two_row = exchange(slices, "col")
    updated = call(third_kernel, tile, [], place, pattern, two_row, high, low, iterate, on_chip=(2, 3, 4))
    return (margin, updated)


def solution(mesh):
    in_specs = (P(None, "row"), P(), P("row", "col"))
    out_specs = (P("row", "col"), P("row", "col"))
    return jax.shard_map(stages, mesh=mesh, in_specs=in_specs, out_specs=out_specs, check_vma=False)
```

```python
import jax
import jax.numpy as jnp
from jax import lax
from jax.experimental import pallas as pl
from jax.experimental.pallas import tpu as pltpu
from jax.sharding import PartitionSpec as P


BLOCK = 128
PRIMS = 3
NB = 32
FIELDS = 3 + 2 * PRIMS
CHUNK = 64
LOG2E = 1.4426950408889634
VMEM = pltpu.VMEM
SMEM = pltpu.SMEM


def split(value):
    high = value.astype(jnp.bfloat16)
    low = (value - high.astype(jnp.float32)).astype(jnp.bfloat16)
    return high, low


def half_tile(fields_ref, left_ref, tile_ref, half, block):
    right = [fields_ref[f, pl.ds(block, 1), :] for f in range(FIELDS)]

    def chunk(step, carry):
        rows = pl.ds(pl.multiple_of(step * CHUNK, CHUNK), CHUNK)
        left = [left_ref[half, f, rows, :] for f in range(FIELDS)]
        distance = (left[0] - right[0]) ** 2
        distance = distance + (left[1] - right[1]) ** 2
        distance = (distance + (left[2] - right[2]) ** 2) * -LOG2E
        total = jnp.zeros_like(distance)
        for p in range(PRIMS):
            stretched = left[3 + p] * distance
            for q in range(PRIMS):
                inverse_root = lax.rsqrt(left[3 + p] + right[3 + q])
                root = (left[6 + p] * inverse_root) * right[6 + q]
                decay = jnp.exp2((stretched * (inverse_root * inverse_root)) * right[3 + q])
                total = total + ((root * root) * root) * decay
        tile_ref[rows, :] = total
        return carry

    lax.fori_loop(0, BLOCK // CHUNK, chunk, 0)


def slot(core, block):
    return (core ^ (block % 2)) * (NB // 2) + block // 2


def spread_own(fields, left, core, col):
    for half in range(2):
        for f in range(FIELDS):
            own = fields[f, pl.ds(slot(core, 2 * col + half), 1), :]
            left[half, f] = jnp.broadcast_to(own, (BLOCK, BLOCK)).T


def tiles_kernel(place, pattern, records, fields, high, low, left, tile):
    row, col = place[0], place[1]
    core = row % 2
    for part in range(2):
        half_table = slice(part * NB // 2, (part + 1) * NB // 2)
        exponents = [records[:, part, 3 + p, :] for p in range(PRIMS)]
        coefficients = [records[:, part, 3 + PRIMS + p, :] for p in range(PRIMS)]
        roots = [jnp.sqrt(e) for e in exponents]
        norm = jnp.zeros_like(exponents[0])
        for p in range(PRIMS):
            for q in range(PRIMS):
                ratio = 2.0 * roots[p] * roots[q] / (exponents[p] + exponents[q])
                norm = norm + coefficients[p] * coefficients[q] * (ratio * jnp.sqrt(ratio))
        scale = (2.0**0.75) * lax.rsqrt(norm)
        for f in range(3):
            fields[f, half_table] = records[:, part, f, :]
        for p in range(PRIMS):
            weight = jnp.exp2(jnp.log2(coefficients[p] * scale) * (1.0 / 3.0))
            fields[3 + p, half_table] = exponents[p]
            fields[6 + p, half_table] = weight * jnp.sqrt(roots[p])
    spread_own(fields, left, core, col)

    def step(index, carry):
        half, block = index // NB, index % NB
        own = 2 * col + half
        needed = pattern[own, block] * pattern[block, row] * pattern[row, own]
        rows = pl.ds(pl.multiple_of(block * BLOCK, BLOCK), BLOCK)
        lanes = pl.ds(pl.multiple_of(half * BLOCK, BLOCK), BLOCK)

        @pl.when(needed != 0)
        def _():
            half_tile(fields, left, tile, half, slot(core, block))
            high[rows, lanes], low[rows, lanes] = split(tile[...].T)

        @pl.when(needed == 0)
        def _():
            high[rows, lanes] = jnp.zeros((BLOCK, BLOCK), jnp.bfloat16)
            low[rows, lanes] = jnp.zeros((BLOCK, BLOCK), jnp.bfloat16)

        return carry

    lax.fori_loop(0, 2 * NB, step, 0)


def margin_kernel(place, pattern, fields, margin, left, tile):
    row, col = place[0], place[1]
    spread_own(fields, left, row % 2, col)
    for half in range(2):
        margin_live = pattern[row, 2 * col + half] != 0
        lanes = slice(half * BLOCK, (half + 1) * BLOCK)

        @pl.when(margin_live)
        def _():
            half_tile(fields, left, tile, half, slot(row % 2, row))
            margin[:, lanes] = tile[...].T

        @pl.when(jnp.logical_not(margin_live))
        def _():
            margin[:, lanes] = jnp.zeros((BLOCK, BLOCK), jnp.float32)


def first_kernel(place, pattern, iterate_row, high, low, product_one):
    total = contract([iterate_row[k] for k in range(16)], high, low)
    for copy in range(16):
        product_one[copy] = total


def replicate_kernel(place, pattern, value, copies):
    for copy in range(copies.shape[0]):
        copies[copy] = value[...]


def prepare_kernel(place, pattern, iterate_col, high, low):
    col = place[1]

    def step(block, carry):
        rows = pl.ds(pl.multiple_of(block * BLOCK, BLOCK), BLOCK)
        for half in range(2):
            lanes = slice(half * BLOCK, (half + 1) * BLOCK)
            mask = (pattern[block, 2 * col + half] != 0).astype(jnp.float32)
            high[rows, lanes], low[rows, lanes] = split(mask * iterate_col[rows, lanes])
        return carry

    lax.fori_loop(0, NB, step, 0)


def contract(pieces, high, low):
    total = jnp.zeros((BLOCK, 2 * BLOCK), jnp.float32)
    for k, piece in enumerate(pieces):
        rows = slice(2 * BLOCK * k, 2 * BLOCK * (k + 1))
        piece_high, piece_low = split(piece)
        total = total + jnp.dot(piece_high, high[rows], preferred_element_type=jnp.float32)
        total = total + jnp.dot(piece_high, low[rows], preferred_element_type=jnp.float32)
        total = total + jnp.dot(piece_low, high[rows], preferred_element_type=jnp.float32)
    return total


def live(pattern, row, column):
    return (pattern[row, column] != 0).astype(jnp.float32)


def second_kernel(place, pattern, one_row, high, low, kept, given, tile):
    row, col = place[0], place[1]
    total = contract([one_row[k] for k in range(16)], high, low)
    for half in range(2):
        own = total[:, half * BLOCK : (half + 1) * BLOCK]
        tile[half] = (live(pattern, row, 2 * col + half) * own).T
    core = row % 2
    kept[...] = tile[core].reshape(BLOCK // 8, 8, BLOCK)
    given[...] = tile[1 - core].reshape(BLOCK // 8, 8, BLOCK)


def third_kernel(place, pattern, two_row, high, low, iterate, updated):
    row, col = place[0], place[1]
    core = row % 2
    pieces = []
    for k in range(16):
        pair = [two_row[:, k, core ^ h].reshape(BLOCK, BLOCK) for h in range(2)]
        pieces.append(jnp.concatenate(pair, axis=1))
    total = contract(pieces, high, low)
    for half in range(2):
        lanes = slice(half * BLOCK, (half + 1) * BLOCK)
        mask = live(pattern, row, 2 * col + half)
        updated[:, lanes] = mask * (1.5 * iterate[:, lanes] - 0.5 * total[:, lanes])


def exchange(pieces, axis):
    return lax.all_to_all(pieces, axis, 0, 0, tiled=True)


def call(kernel, out_shapes, scratch, *operands, on_chip=()):
    whole = pl.BlockSpec(memory_space=VMEM)
    scalars = pl.BlockSpec(memory_space=SMEM)
    operands = list(operands)
    for k in on_chip:
        operands[k] = pltpu.with_memory_space_constraint(operands[k], VMEM)
    return pl.pallas_call(
        kernel,
        out_shape=out_shapes,
        in_specs=[scalars, scalars] + [whole] * (len(operands) - 2),
        out_specs=jax.tree.map(lambda _: whole, out_shapes),
        scratch_shapes=scratch,
        compiler_params=pltpu.CompilerParams(vmem_limit_bytes=24 * 2**20),
    )(*operands)


def stages(records, pattern, iterate):
    place = jnp.stack([lax.axis_index("row"), lax.axis_index("col")]).astype(jnp.int32)
    tile = jax.ShapeDtypeStruct((BLOCK, 2 * BLOCK), jnp.float32)
    panel = VMEM((NB * BLOCK, 2 * BLOCK), jnp.bfloat16)
    tiles = jax.ShapeDtypeStruct((16, BLOCK, 2 * BLOCK), jnp.float32)
    iterate_col = lax.all_gather(iterate, "row", axis=0, tiled=True)
    cores = [[2 * z + core for z in range(16)] for core in range(2)]
    partner = [(r, r ^ 1) for r in range(NB)]
    left = VMEM((2, FIELDS, BLOCK, BLOCK), jnp.float32)
    square = VMEM((BLOCK, BLOCK), jnp.float32)
    table = VMEM((FIELDS, NB, BLOCK), jnp.float32)
    both = jnp.stack([records, lax.ppermute(records, "row", partner)])
    everyone = lax.all_gather(both, "row", axis=0, axis_index_groups=cores)
    iterate_row = exchange(jnp.broadcast_to(iterate[None], tiles.shape), "col")
    fields, margin_high, margin_low = call(
        tiles_kernel, (table, panel, panel), [left, square], place, pattern, everyone
    )
    product_one = call(first_kernel, tiles, [], place, pattern, iterate_row, margin_high, margin_low, on_chip=(2, 3, 4))
    margin = call(margin_kernel, tile, [left, square], place, pattern, fields, on_chip=(2,))
    one_row = exchange(product_one, "col")
    high, low = call(prepare_kernel, (panel, panel), [], place, pattern, iterate_col)
    half = VMEM((16, 8, BLOCK), jnp.float32)
    turned = VMEM((2, BLOCK, BLOCK), jnp.float32)
    kept, given = call(
        second_kernel, (half, half), [turned], place, pattern, one_row, high, low, on_chip=(2, 3, 4)
    )
    given = lax.ppermute(given, "row", partner)
    slices = jnp.stack([kept, given], axis=1)
    slices = exchange(slices, "col")
    slices = lax.all_to_all(slices, "row", 0, 0, tiled=True, axis_index_groups=cores)
    copies = VMEM((16,) + slices.shape, jnp.float32)
    slices = call(replicate_kernel, copies, [], place, pattern, slices, on_chip=(2,))
    two_row = exchange(slices, "col")
    updated = call(third_kernel, tile, [], place, pattern, two_row, high, low, iterate, on_chip=(2, 3, 4))
    return (margin, updated)


def solution(mesh):
    in_specs = (P(None, "row"), P(), P("row", "col"))
    out_specs = (P("row", "col"), P("row", "col"))
    return jax.shard_map(stages, mesh=mesh, in_specs=in_specs, out_specs=out_specs, check_vma=False)
```

```python
import jax
import jax.numpy as jnp
from jax import lax
from jax.experimental import pallas as pl
from jax.experimental.pallas import tpu as pltpu
from jax.sharding import PartitionSpec as P


BLOCK = 128
PRIMS = 3
NB = 32
FIELDS = 3 + 2 * PRIMS
CHUNK = 64
LOG2E = 1.4426950408889634
VMEM = pltpu.VMEM
SMEM = pltpu.SMEM
HBM = pltpu.HBM


def split(value):
    high = value.astype(jnp.bfloat16)
    low = (value - high.astype(jnp.float32)).astype(jnp.bfloat16)
    return high, low


def half_tile(fields_ref, left_ref, tile_ref, half, block):
    right = [fields_ref[f, pl.ds(block, 1), :] for f in range(FIELDS)]

    def chunk(step, carry):
        rows = pl.ds(pl.multiple_of(step * CHUNK, CHUNK), CHUNK)
        left = [left_ref[half, f, rows, :] for f in range(FIELDS)]
        distance = (left[0] - right[0]) ** 2
        distance = distance + (left[1] - right[1]) ** 2
        distance = (distance + (left[2] - right[2]) ** 2) * -LOG2E
        total = jnp.zeros_like(distance)
        for p in range(PRIMS):
            stretched = left[3 + p] * distance
            for q in range(PRIMS):
                inverse_root = lax.rsqrt(left[3 + p] + right[3 + q])
                root = (left[6 + p] * inverse_root) * right[6 + q]
                decay = jnp.exp2((stretched * (inverse_root * inverse_root)) * right[3 + q])
                total = total + ((root * root) * root) * decay
        tile_ref[rows, :] = total
        return carry

    lax.fori_loop(0, BLOCK // CHUNK, chunk, 0)


def slot(core, block):
    return (core ^ (block % 2)) * (NB // 2) + block // 2


def spread_own(fields, left, core, col):
    for half in range(2):
        for f in range(FIELDS):
            own = fields[f, pl.ds(slot(core, 2 * col + half), 1), :]
            left[half, f] = jnp.broadcast_to(own, (BLOCK, BLOCK)).T


def send_copies(tile, copies, sems):
    moves = [pltpu.make_async_copy(tile, copies.at[k], sems.at[k]) for k in range(16)]
    for move in moves:
        move.start()
    for move in moves:
        move.wait()


def first_kernel(place, pattern, records, iterate_row, fields, copies, left, tile, high, low, one, sems):
    row, col = place[0], place[1]
    core = row % 2
    for part in range(2):
        half_table = slice(part * NB // 2, (part + 1) * NB // 2)
        exponents = [records[:, part, 3 + p, :] for p in range(PRIMS)]
        coefficients = [records[:, part, 3 + PRIMS + p, :] for p in range(PRIMS)]
        roots = [jnp.sqrt(e) for e in exponents]
        norm = jnp.zeros_like(exponents[0])
        for p in range(PRIMS):
            for q in range(PRIMS):
                ratio = 2.0 * roots[p] * roots[q] / (exponents[p] + exponents[q])
                norm = norm + coefficients[p] * coefficients[q] * (ratio * jnp.sqrt(ratio))
        scale = (2.0**0.75) * lax.rsqrt(norm)
        for f in range(3):
            fields[f, half_table] = records[:, part, f, :]
        for p in range(PRIMS):
            weight = jnp.exp2(jnp.log2(coefficients[p] * scale) * (1.0 / 3.0))
            fields[3 + p, half_table] = exponents[p]
            fields[6 + p, half_table] = weight * jnp.sqrt(roots[p])
    spread_own(fields, left, core, col)

    def step(index, carry):
        half, block = index // NB, index % NB
        own = 2 * col + half
        needed = pattern[own, block] * pattern[block, row] * pattern[row, own]
        rows = pl.ds(pl.multiple_of(block * BLOCK, BLOCK), BLOCK)
        lanes = pl.ds(pl.multiple_of(half * BLOCK, BLOCK), BLOCK)

        @pl.when(needed != 0)
        def _():
            half_tile(fields, left, tile, half, slot(core, block))
            high[rows, lanes], low[rows, lanes] = split(tile[...].T)

        @pl.when(needed == 0)
        def _():
            high[rows, lanes] = jnp.zeros((BLOCK, BLOCK), jnp.bfloat16)
            low[rows, lanes] = jnp.zeros((BLOCK, BLOCK), jnp.bfloat16)

        return carry

    lax.fori_loop(0, 2 * NB, step, 0)
    one[...] = contract([iterate_row[k] for k in range(16)], high, low)
    send_copies(one, copies, sems)


def margin_kernel(place, pattern, fields, margin, left, tile):
    row, col = place[0], place[1]
    spread_own(fields, left, row % 2, col)
    for half in range(2):
        margin_live = pattern[row, 2 * col + half] != 0
        lanes = slice(half * BLOCK, (half + 1) * BLOCK)

        @pl.when(margin_live)
        def _():
            half_tile(fields, left, tile, half, slot(row % 2, row))
            margin[:, lanes] = tile[...].T

        @pl.when(jnp.logical_not(margin_live))
        def _():
            margin[:, lanes] = jnp.zeros((BLOCK, BLOCK), jnp.float32)


def hbm_copies_kernel(value, copies, sems):
    send_copies(value, copies, sems)


def replicate_kernel(value, copies):
    for copy in range(copies.shape[0]):
        copies[copy] = value[...]


def prepare_kernel(place, pattern, iterate_col, high, low):
    col = place[1]

    def step(block, carry):
        rows = pl.ds(pl.multiple_of(block * BLOCK, BLOCK), BLOCK)
        for half in range(2):
            lanes = slice(half * BLOCK, (half + 1) * BLOCK)
            mask = (pattern[block, 2 * col + half] != 0).astype(jnp.float32)
            high[rows, lanes], low[rows, lanes] = split(mask * iterate_col[rows, lanes])
        return carry

    lax.fori_loop(0, NB, step, 0)


def contract(pieces, high, low):
    total = jnp.zeros((BLOCK, 2 * BLOCK), jnp.float32)
    for k, piece in enumerate(pieces):
        rows = slice(2 * BLOCK * k, 2 * BLOCK * (k + 1))
        piece_high, piece_low = split(piece)
        total = total + jnp.dot(piece_high, high[rows], preferred_element_type=jnp.float32)
        total = total + jnp.dot(piece_high, low[rows], preferred_element_type=jnp.float32)
        total = total + jnp.dot(piece_low, high[rows], preferred_element_type=jnp.float32)
    return total


def live(pattern, row, column):
    return (pattern[row, column] != 0).astype(jnp.float32)


def second_kernel(place, pattern, one_row, high, low, kept, given, tile):
    row, col = place[0], place[1]
    total = contract([one_row[k] for k in range(16)], high, low)
    for half in range(2):
        own = total[:, half * BLOCK : (half + 1) * BLOCK]
        tile[half] = (live(pattern, row, 2 * col + half) * own).T
    core = row % 2
    kept[...] = tile[core].reshape(BLOCK // 8, 8, BLOCK)
    given[...] = tile[1 - core].reshape(BLOCK // 8, 8, BLOCK)


def third_kernel(place, pattern, two_row, high, low, iterate, updated):
    row, col = place[0], place[1]
    core = row % 2
    pieces = []
    for k in range(16):
        pair = [two_row[:, k, core ^ h].reshape(BLOCK, BLOCK) for h in range(2)]
        pieces.append(jnp.concatenate(pair, axis=1))
    total = contract(pieces, high, low)
    for half in range(2):
        lanes = slice(half * BLOCK, (half + 1) * BLOCK)
        mask = live(pattern, row, 2 * col + half)
        updated[:, lanes] = mask * (1.5 * iterate[:, lanes] - 0.5 * total[:, lanes])


def exchange(pieces, axis):
    return lax.all_to_all(pieces, axis, 0, 0, tiled=True)


def call(kernel, out_shapes, scratch, *operands, on_chip=(), outs=None, scalars=2):
    whole = pl.BlockSpec(memory_space=VMEM)
    in_specs = [pl.BlockSpec(memory_space=SMEM)] * scalars + [whole] * (len(operands) - scalars)
    operands = list(operands)
    for k in on_chip:
        operands[k] = pltpu.with_memory_space_constraint(operands[k], VMEM)
    if outs is None:
        out_specs = jax.tree.map(lambda _: whole, out_shapes)
    else:
        out_specs = tuple(pl.BlockSpec(memory_space=space) for space in outs)
        out_specs = out_specs if isinstance(out_shapes, tuple) else out_specs[0]
    return pl.pallas_call(
        kernel,
        out_shape=out_shapes,
        in_specs=in_specs,
        out_specs=out_specs,
        scratch_shapes=scratch,
        compiler_params=pltpu.CompilerParams(vmem_limit_bytes=24 * 2**20),
    )(*operands)


def stages(records, pattern, iterate):
    place = jnp.stack([lax.axis_index("row"), lax.axis_index("col")]).astype(jnp.int32)
    tile = jax.ShapeDtypeStruct((BLOCK, 2 * BLOCK), jnp.float32)
    panel = VMEM((NB * BLOCK, 2 * BLOCK), jnp.bfloat16)
    tiles = HBM((16, BLOCK, 2 * BLOCK), jnp.float32)
    iterate_col = lax.all_gather(iterate, "row", axis=0, tiled=True)
    cores = [[2 * z + core for z in range(16)] for core in range(2)]
    partner = [(r, r ^ 1) for r in range(NB)]
    left = VMEM((2, FIELDS, BLOCK, BLOCK), jnp.float32)
    square = VMEM((BLOCK, BLOCK), jnp.float32)
    table = VMEM((FIELDS, NB, BLOCK), jnp.float32)
    both = jnp.stack([records, lax.ppermute(records, "row", partner)])
    everyone = lax.all_gather(both, "row", axis=0, axis_index_groups=cores)
    sems = pltpu.SemaphoreType.DMA((16,))
    copies = call(hbm_copies_kernel, tiles, [sems], iterate, outs=(HBM,), scalars=0)
    iterate_row = exchange(copies, "col")
    fields, product_one = call(
        first_kernel,
        (table, tiles),
        [left, square, panel, panel, VMEM((BLOCK, 2 * BLOCK), jnp.float32), sems],
        place,
        pattern,
        everyone,
        iterate_row,
        on_chip=(2, 3),
        outs=(VMEM, HBM),
    )
    margin = call(margin_kernel, tile, [left, square], place, pattern, fields, on_chip=(2,))
    one_row = exchange(product_one, "col")
    high, low = call(prepare_kernel, (panel, panel), [], place, pattern, iterate_col)
    half = VMEM((16, 8, BLOCK), jnp.float32)
    turned = VMEM((2, BLOCK, BLOCK), jnp.float32)
    kept, given = call(
        second_kernel, (half, half), [turned], place, pattern, one_row, high, low, on_chip=(2, 3, 4)
    )
    given = lax.ppermute(given, "row", partner)
    slices = jnp.stack([kept, given], axis=1)
    slices = exchange(slices, "col")
    slices = lax.all_to_all(slices, "row", 0, 0, tiled=True, axis_index_groups=cores)
    copies = VMEM((16,) + slices.shape, jnp.float32)
    slices = call(replicate_kernel, copies, [], slices, on_chip=(0,), scalars=0)
    two_row = exchange(slices, "col")
    updated = call(third_kernel, tile, [], place, pattern, two_row, high, low, iterate, on_chip=(2, 3, 4))
    return (margin, updated)


def solution(mesh):
    in_specs = (P(None, "row"), P(), P("row", "col"))
    out_specs = (P("row", "col"), P("row", "col"))
    return jax.shard_map(stages, mesh=mesh, in_specs=in_specs, out_specs=out_specs, check_vma=False)
```

```python
import jax
import jax.numpy as jnp
from jax import lax
from jax.experimental import pallas as pl
from jax.experimental.pallas import tpu as pltpu
from jax.sharding import PartitionSpec as P


BLOCK = 128
PRIMS = 3
NB = 32
FIELDS = 3 + 2 * PRIMS
CHUNK = 128
PANEL = 512
PART = 1024
LOG2E = 1.4426950408889634
VMEM = pltpu.VMEM
SMEM = pltpu.SMEM
HBM = pltpu.HBM


def split(value):
    high = value.astype(jnp.bfloat16)
    low = (value - high.astype(jnp.float32)).astype(jnp.bfloat16)
    return high, low


def dot_transposed(left, right):
    return lax.dot_general(left, right, (((1,), (1,)), ((), ())), preferred_element_type=jnp.float32)


def half_tile(fields_ref, left_ref, tile_ref, half, block):
    right = [fields_ref[f, pl.ds(block, 1), :] for f in range(FIELDS)]

    def chunk(step, carry):
        rows = pl.ds(pl.multiple_of(step * CHUNK, CHUNK), CHUNK)
        left = [left_ref[half, f, rows, :] for f in range(FIELDS)]
        distance = (left[0] - right[0]) ** 2
        distance = distance + (left[1] - right[1]) ** 2
        distance = (distance + (left[2] - right[2]) ** 2) * -LOG2E
        total = jnp.zeros_like(distance)
        for p in range(PRIMS):
            stretched = left[3 + p] * distance
            for q in range(PRIMS):
                inverse_root = lax.rsqrt(left[3 + p] + right[3 + q])
                root = (left[6 + p] * inverse_root) * right[6 + q]
                decay = jnp.exp2((stretched * (inverse_root * inverse_root)) * right[3 + q])
                total = total + ((root * root) * root) * decay
        tile_ref[rows, :] = total
        return carry

    lax.fori_loop(0, BLOCK // CHUNK, chunk, 0)


def slot(core, block):
    return (core ^ (block % 2)) * (NB // 2) + block // 2


def spread_own(fields, left, core, col):
    for half in range(2):
        for f in range(FIELDS):
            own = fields[f, pl.ds(slot(core, 2 * col + half), 1), :]
            left[half, f] = jnp.broadcast_to(own, (BLOCK, BLOCK)).T


def send_copies(tile, copies, sems):
    moves = [pltpu.make_async_copy(tile, copies.at[k], sems.at[k]) for k in range(16)]
    for move in moves:
        move.start()
    for move in moves:
        move.wait()


def first_kernel(place, pattern, records, iterate_row, fields, copies, left, tile, high, low, one, sems):
    row, col = place[0], place[1]
    core = row % 2
    for part in range(2):
        half_table = slice(part * NB // 2, (part + 1) * NB // 2)
        exponents = [records[:, part, 3 + p, :] for p in range(PRIMS)]
        coefficients = [records[:, part, 3 + PRIMS + p, :] for p in range(PRIMS)]
        roots = [jnp.sqrt(e) for e in exponents]
        norm = jnp.zeros_like(exponents[0])
        for p in range(PRIMS):
            for q in range(PRIMS):
                ratio = 2.0 * roots[p] * roots[q] / (exponents[p] + exponents[q])
                norm = norm + coefficients[p] * coefficients[q] * (ratio * jnp.sqrt(ratio))
        scale = (2.0**0.75) * lax.rsqrt(norm)
        for f in range(3):
            fields[f, half_table] = records[:, part, f, :]
        for p in range(PRIMS):
            weight = jnp.exp2(jnp.log2(coefficients[p] * scale) * (1.0 / 3.0))
            fields[3 + p, half_table] = exponents[p]
            fields[6 + p, half_table] = weight * jnp.sqrt(roots[p])
    spread_own(fields, left, core, col)

    def step(index, carry):
        half, block = index // NB, index % NB
        own = 2 * col + half
        needed = pattern[own, block] * pattern[block, row] * pattern[row, own]
        rows = pl.ds(pl.multiple_of(block * BLOCK, BLOCK), BLOCK)
        lanes = pl.ds(pl.multiple_of(half * BLOCK, BLOCK), BLOCK)

        @pl.when(needed != 0)
        def _():
            half_tile(fields, left, tile, half, slot(core, block))
            high[lanes, rows], low[lanes, rows] = split(tile[...])

        @pl.when(needed == 0)
        def _():
            high[lanes, rows] = jnp.zeros((BLOCK, BLOCK), jnp.bfloat16)
            low[lanes, rows] = jnp.zeros((BLOCK, BLOCK), jnp.bfloat16)

        return carry

    lax.fori_loop(0, 2 * NB, step, 0)
    total = jnp.zeros((BLOCK, 2 * BLOCK), jnp.float32)
    for k in range(16):
        columns = slice(2 * BLOCK * k, 2 * BLOCK * (k + 1))
        piece_high, piece_low = split(iterate_row[k])
        total = total + dot_transposed(piece_high, high[:, columns])
        total = total + dot_transposed(piece_high, low[:, columns])
        total = total + dot_transposed(piece_low, high[:, columns])
    one[...] = total
    send_copies(one, copies, sems)


def margin_kernel(place, pattern, fields, margin, left, tile):
    row, col = place[0], place[1]
    spread_own(fields, left, row % 2, col)
    for half in range(2):
        margin_live = pattern[row, 2 * col + half] != 0
        lanes = slice(half * BLOCK, (half + 1) * BLOCK)

        @pl.when(margin_live)
        def _():
            half_tile(fields, left, tile, half, slot(row % 2, row))
            margin[:, lanes] = tile[...].T

        @pl.when(jnp.logical_not(margin_live))
        def _():
            margin[:, lanes] = jnp.zeros((BLOCK, BLOCK), jnp.float32)


def hbm_copies_kernel(value, copies, sems):
    send_copies(value, copies, sems)


def replicate_kernel(value, copies):
    for copy in range(copies.shape[0]):
        copies[copy] = value[...]


def prepare_kernel(place, pattern, iterate_col, high, low):
    col = place[1]
    first = pl.program_id(0) * (PANEL // BLOCK)
    for block in range(PANEL // BLOCK):
        rows = slice(block * BLOCK, (block + 1) * BLOCK)
        for half in range(2):
            lanes = slice(half * BLOCK, (half + 1) * BLOCK)
            mask = live(pattern, first + block, 2 * col + half)
            high[rows, lanes], low[rows, lanes] = split(mask * iterate_col[rows, lanes])


def contract(pieces, high, low):
    total = jnp.zeros((BLOCK, 2 * BLOCK), jnp.float32)
    for k, piece in enumerate(pieces):
        rows = slice(2 * BLOCK * k, 2 * BLOCK * (k + 1))
        piece_high, piece_low = split(piece)
        total = total + jnp.dot(piece_high, high[rows], preferred_element_type=jnp.float32)
        total = total + jnp.dot(piece_high, low[rows], preferred_element_type=jnp.float32)
        total = total + jnp.dot(piece_low, high[rows], preferred_element_type=jnp.float32)
    return total


def live(pattern, row, column):
    return (pattern[row, column] != 0).astype(jnp.float32)


def second_kernel(place, pattern, one_row, high, low, kept, given, total, tile):
    row, col = place[0], place[1]
    part = pl.program_id(0)
    pieces = PART // (2 * BLOCK)
    product = contract([one_row[part * pieces + k] for k in range(pieces)], high, low)

    @pl.when(part == 0)
    def _():
        total[...] = product

    @pl.when(part > 0)
    def _():
        total[...] += product

    @pl.when(part == pl.num_programs(0) - 1)
    def _():
        for half in range(2):
            own = total[:, half * BLOCK : (half + 1) * BLOCK]
            tile[half] = (live(pattern, row, 2 * col + half) * own).T
        core = row % 2
        kept[...] = tile[core].reshape(BLOCK // 8, 8, BLOCK)
        given[...] = tile[1 - core].reshape(BLOCK // 8, 8, BLOCK)


def third_kernel(place, pattern, two_row, high, low, iterate, updated):
    row, col = place[0], place[1]
    core = row % 2
    pieces = []
    for k in range(16):
        pair = [two_row[:, k, core ^ h].reshape(BLOCK, BLOCK) for h in range(2)]
        pieces.append(jnp.concatenate(pair, axis=1))
    total = contract(pieces, high, low)
    for half in range(2):
        lanes = slice(half * BLOCK, (half + 1) * BLOCK)
        mask = live(pattern, row, 2 * col + half)
        updated[:, lanes] = mask * (1.5 * iterate[:, lanes] - 0.5 * total[:, lanes])


def exchange(pieces, axis):
    return lax.all_to_all(pieces, axis, 0, 0, tiled=True)


def call(kernel, out_shapes, scratch, *operands, on_chip=(), outs=None, scalars=2, grid=(), blocks=None, source=VMEM, stay=()):
    whole = pl.BlockSpec(memory_space=VMEM)
    in_specs = [pl.BlockSpec(memory_space=SMEM)] * scalars + [pl.BlockSpec(memory_space=source)] * (
        len(operands) - scalars
    )
    blocks = blocks or {}
    for k, block in blocks.items():
        if k < len(operands):
            in_specs[k] = pl.BlockSpec(block, lambda i: (i, 0))
    operands = list(operands)
    for k in on_chip:
        operands[k] = pltpu.with_memory_space_constraint(operands[k], VMEM)
    for k in stay:
        operands[k] = pltpu.with_memory_space_constraint(operands[k], HBM)
    if outs is None:
        out_specs = jax.tree.map(lambda _: whole, out_shapes)
    else:
        out_specs = tuple(
            pl.BlockSpec(space, lambda i: (i, 0)) if isinstance(space, tuple) else pl.BlockSpec(memory_space=space)
            for space in outs
        )
        out_specs = out_specs if isinstance(out_shapes, tuple) else out_specs[0]
    return pl.pallas_call(
        kernel,
        out_shape=out_shapes,
        grid=grid,
        in_specs=in_specs,
        out_specs=out_specs,
        scratch_shapes=scratch,
        compiler_params=pltpu.CompilerParams(vmem_limit_bytes=24 * 2**20),
    )(*operands)


def stages(records, pattern, iterate):
    place = jnp.stack([lax.axis_index("row"), lax.axis_index("col")]).astype(jnp.int32)
    tile = jax.ShapeDtypeStruct((BLOCK, 2 * BLOCK), jnp.float32)
    stored = HBM((NB * BLOCK, 2 * BLOCK), jnp.bfloat16)
    tiles = HBM((16, BLOCK, 2 * BLOCK), jnp.float32)
    iterate_col = lax.all_gather(iterate, "row", axis=0, tiled=True)
    cores = [[2 * z + core for z in range(16)] for core in range(2)]
    partner = [(r, r ^ 1) for r in range(NB)]
    left = VMEM((2, FIELDS, BLOCK, BLOCK), jnp.float32)
    square = VMEM((BLOCK, BLOCK), jnp.float32)
    table = VMEM((FIELDS, NB, BLOCK), jnp.float32)
    both = jnp.stack([records, lax.ppermute(records, "row", partner)])
    everyone = lax.all_gather(both, "row", axis=0, axis_index_groups=cores)
    sems = pltpu.SemaphoreType.DMA((16,))
    wide = VMEM((2 * BLOCK, NB * BLOCK), jnp.bfloat16)
    copies = call(
        hbm_copies_kernel, tiles, [sems], iterate, outs=(HBM,), scalars=0, source=HBM, stay=(0,)
    )
    iterate_row = exchange(copies, "col")
    fields, product_one = call(
        first_kernel,
        (table, tiles),
        [left, square, wide, wide, VMEM((BLOCK, 2 * BLOCK), jnp.float32), sems],
        place,
        pattern,
        everyone,
        iterate_row,
        on_chip=(2, 3),
        outs=(VMEM, HBM),
    )
    margin = call(margin_kernel, tile, [left, square], place, pattern, fields, on_chip=(2,))
    one_row = exchange(product_one, "col")
    window = (PANEL, 2 * BLOCK)
    high, low = call(
        prepare_kernel,
        (stored, stored),
        [],
        place,
        pattern,
        iterate_col,
        outs=(window, window),
        grid=(NB * BLOCK // PANEL,),
        blocks={2: window},
        stay=(2,),
    )
    half = VMEM((16, 8, BLOCK), jnp.float32)
    turned = VMEM((2, BLOCK, BLOCK), jnp.float32)
    window = (PART, 2 * BLOCK)
    kept, given = call(
        second_kernel,
        (half, half),
        [VMEM((BLOCK, 2 * BLOCK), jnp.float32), turned],
        place,
        pattern,
        one_row,
        high,
        low,
        on_chip=(2,),
        grid=(NB * BLOCK // PART,),
        blocks={3: window, 4: window},
        stay=(3, 4),
    )
    given = lax.ppermute(given, "row", partner)
    slices = jnp.stack([kept, given], axis=1)
    slices = exchange(slices, "col")
    slices = lax.all_to_all(slices, "row", 0, 0, tiled=True, axis_index_groups=cores)
    copies = VMEM((16,) + slices.shape, jnp.float32)
    slices = call(replicate_kernel, copies, [], slices, on_chip=(0,), scalars=0)
    two_row = exchange(slices, "col")
    updated = call(third_kernel, tile, [], place, pattern, two_row, high, low, iterate, on_chip=(2, 3, 4))
    return (margin, updated)


def solution(mesh):
    in_specs = (P(None, "row"), P(), P("row", "col"))
    out_specs = (P("row", "col"), P("row", "col"))
    return jax.shard_map(stages, mesh=mesh, in_specs=in_specs, out_specs=out_specs, check_vma=False)
```

```python
import jax
import jax.numpy as jnp
from jax import lax
from jax.experimental import pallas as pl
from jax.experimental.pallas import tpu as pltpu
from jax.sharding import PartitionSpec as P


BLOCK = 128
PRIMS = 3
NB = 32
FIELDS = 3 + 2 * PRIMS
CHUNK = 128
PANEL = 1024
PART = 1024
LOG2E = 1.4426950408889634
VMEM = pltpu.VMEM
SMEM = pltpu.SMEM
HBM = pltpu.HBM


def split(value):
    high = value.astype(jnp.bfloat16)
    low = (value - high.astype(jnp.float32)).astype(jnp.bfloat16)
    return high, low


def dot_transposed(left, right):
    return lax.dot_general(left, right, (((1,), (1,)), ((), ())), preferred_element_type=jnp.float32)


def half_tile(fields_ref, left_ref, tile_ref, half, block):
    right = [fields_ref[f, pl.ds(block, 1), :] for f in range(FIELDS)]

    def chunk(step, carry):
        rows = pl.ds(pl.multiple_of(step * CHUNK, CHUNK), CHUNK)
        left = [left_ref[half, f, rows, :] for f in range(FIELDS)]
        distance = (left[0] - right[0]) ** 2
        distance = distance + (left[1] - right[1]) ** 2
        distance = (distance + (left[2] - right[2]) ** 2) * -LOG2E
        total = jnp.zeros_like(distance)
        for p in range(PRIMS):
            stretched = left[3 + p] * distance
            for q in range(PRIMS):
                inverse_root = lax.rsqrt(left[3 + p] + right[3 + q])
                root = (left[6 + p] * inverse_root) * right[6 + q]
                decay = jnp.exp2((stretched * (inverse_root * inverse_root)) * right[3 + q])
                total = total + ((root * root) * root) * decay
        tile_ref[rows, :] = total
        return carry

    lax.fori_loop(0, BLOCK // CHUNK, chunk, 0)


def slot(core, block):
    return (core ^ (block % 2)) * (NB // 2) + block // 2


def spread_own(fields, left, core, col):
    for half in range(2):
        for f in range(FIELDS):
            own = fields[f, pl.ds(slot(core, 2 * col + half), 1), :]
            left[half, f] = jnp.broadcast_to(own, (BLOCK, BLOCK)).T


def send_copies(tile, copies, sems):
    moves = [pltpu.make_async_copy(tile, copies.at[k], sems.at[k]) for k in range(16)]
    for move in moves:
        move.start()
    for move in moves:
        move.wait()


def first_kernel(place, pattern, records, iterate_row, fields, copies, left, tile, high, low, one, sems):
    row, col = place[0], place[1]
    core = row % 2
    for part in range(2):
        half_table = slice(part * NB // 2, (part + 1) * NB // 2)
        exponents = [records[:, part, 3 + p, :] for p in range(PRIMS)]
        coefficients = [records[:, part, 3 + PRIMS + p, :] for p in range(PRIMS)]
        roots = [jnp.sqrt(e) for e in exponents]
        norm = jnp.zeros_like(exponents[0])
        for p in range(PRIMS):
            for q in range(PRIMS):
                ratio = 2.0 * roots[p] * roots[q] / (exponents[p] + exponents[q])
                norm = norm + coefficients[p] * coefficients[q] * (ratio * jnp.sqrt(ratio))
        scale = (2.0**0.75) * lax.rsqrt(norm)
        for f in range(3):
            fields[f, half_table] = records[:, part, f, :]
        for p in range(PRIMS):
            weight = jnp.exp2(jnp.log2(coefficients[p] * scale) * (1.0 / 3.0))
            fields[3 + p, half_table] = exponents[p]
            fields[6 + p, half_table] = weight * jnp.sqrt(roots[p])
    spread_own(fields, left, core, col)

    def step(index, carry):
        half, block = index // NB, index % NB
        own = 2 * col + half
        needed = pattern[own, block] * pattern[block, row] * pattern[row, own]
        rows = pl.ds(pl.multiple_of(block * BLOCK, BLOCK), BLOCK)
        lanes = pl.ds(pl.multiple_of(half * BLOCK, BLOCK), BLOCK)

        @pl.when(needed != 0)
        def _():
            half_tile(fields, left, tile, half, slot(core, block))
            high[lanes, rows], low[lanes, rows] = split(tile[...])

        @pl.when(needed == 0)
        def _():
            high[lanes, rows] = jnp.zeros((BLOCK, BLOCK), jnp.bfloat16)
            low[lanes, rows] = jnp.zeros((BLOCK, BLOCK), jnp.bfloat16)

        return carry

    lax.fori_loop(0, 2 * NB, step, 0)
    total = jnp.zeros((BLOCK, 2 * BLOCK), jnp.float32)
    for k in range(16):
        columns = slice(2 * BLOCK * k, 2 * BLOCK * (k + 1))
        piece_high, piece_low = split(iterate_row[k])
        total = total + dot_transposed(piece_high, high[:, columns])
        total = total + dot_transposed(piece_high, low[:, columns])
        total = total + dot_transposed(piece_low, high[:, columns])
    one[...] = total
    send_copies(one, copies, sems)


def margin_kernel(place, pattern, fields, margin, left, tile):
    row, col = place[0], place[1]
    spread_own(fields, left, row % 2, col)
    for half in range(2):
        margin_live = pattern[row, 2 * col + half] != 0
        lanes = slice(half * BLOCK, (half + 1) * BLOCK)

        @pl.when(margin_live)
        def _():
            half_tile(fields, left, tile, half, slot(row % 2, row))
            margin[:, lanes] = tile[...].T

        @pl.when(jnp.logical_not(margin_live))
        def _():
            margin[:, lanes] = jnp.zeros((BLOCK, BLOCK), jnp.float32)


def hbm_copies_kernel(value, copies, sems):
    send_copies(value, copies, sems)


def replicate_kernel(value, copies):
    for copy in range(copies.shape[0]):
        copies[copy] = value[...]


def prepare_kernel(place, pattern, iterate_col, high, low):
    col = place[1]
    first = pl.program_id(0) * (PANEL // BLOCK)
    for block in range(PANEL // BLOCK):
        rows = slice(block * BLOCK, (block + 1) * BLOCK)
        for half in range(2):
            lanes = slice(half * BLOCK, (half + 1) * BLOCK)
            mask = live(pattern, first + block, 2 * col + half)
            high[rows, lanes], low[rows, lanes] = split(mask * iterate_col[rows, lanes])


def contract(pieces, high, low):
    total = jnp.zeros((BLOCK, 2 * BLOCK), jnp.float32)
    for k, piece in enumerate(pieces):
        rows = slice(2 * BLOCK * k, 2 * BLOCK * (k + 1))
        piece_high, piece_low = split(piece)
        total = total + jnp.dot(piece_high, high[rows], preferred_element_type=jnp.float32)
        total = total + jnp.dot(piece_high, low[rows], preferred_element_type=jnp.float32)
        total = total + jnp.dot(piece_low, high[rows], preferred_element_type=jnp.float32)
    return total


def live(pattern, row, column):
    return (pattern[row, column] != 0).astype(jnp.float32)


def second_kernel(place, pattern, one_row, high, low, kept, given, total, tile):
    row, col = place[0], place[1]
    part = pl.program_id(0)
    pieces = PART // (2 * BLOCK)
    product = contract([one_row[part * pieces + k] for k in range(pieces)], high, low)

    @pl.when(part == 0)
    def _():
        total[...] = product

    @pl.when(part > 0)
    def _():
        total[...] += product

    @pl.when(part == pl.num_programs(0) - 1)
    def _():
        for half in range(2):
            own = total[:, half * BLOCK : (half + 1) * BLOCK]
            tile[half] = (live(pattern, row, 2 * col + half) * own).T
        core = row % 2
        kept[...] = tile[core].reshape(BLOCK // 8, 8, BLOCK)
        given[...] = tile[1 - core].reshape(BLOCK // 8, 8, BLOCK)


def third_kernel(place, pattern, two_row, high, low, iterate, updated):
    row, col = place[0], place[1]
    core = row % 2
    pieces = []
    for k in range(16):
        pair = [two_row[:, k, core ^ h].reshape(BLOCK, BLOCK) for h in range(2)]
        pieces.append(jnp.concatenate(pair, axis=1))
    total = contract(pieces, high, low)
    for half in range(2):
        lanes = slice(half * BLOCK, (half + 1) * BLOCK)
        mask = live(pattern, row, 2 * col + half)
        updated[:, lanes] = mask * (1.5 * iterate[:, lanes] - 0.5 * total[:, lanes])


def exchange(pieces, axis):
    return lax.all_to_all(pieces, axis, 0, 0, tiled=True)


def call(kernel, out_shapes, scratch, *operands, on_chip=(), outs=None, scalars=2, grid=(), blocks=None, stay=()):
    whole = pl.BlockSpec(memory_space=VMEM)
    in_specs = [pl.BlockSpec(memory_space=SMEM)] * scalars + [whole] * (len(operands) - scalars)
    blocks = blocks or {}
    for k, block in blocks.items():
        if k < len(operands):
            in_specs[k] = pl.BlockSpec(block, lambda i: (i, 0))
    operands = list(operands)
    for k in on_chip:
        operands[k] = pltpu.with_memory_space_constraint(operands[k], VMEM)
    for k in stay:
        operands[k] = pltpu.with_memory_space_constraint(operands[k], HBM)
    if outs is None:
        out_specs = jax.tree.map(lambda _: whole, out_shapes)
    else:
        out_specs = tuple(
            pl.BlockSpec(space, lambda i: (i, 0)) if isinstance(space, tuple) else pl.BlockSpec(memory_space=space)
            for space in outs
        )
        out_specs = out_specs if isinstance(out_shapes, tuple) else out_specs[0]
    return pl.pallas_call(
        kernel,
        out_shape=out_shapes,
        grid=grid,
        in_specs=in_specs,
        out_specs=out_specs,
        scratch_shapes=scratch,
        compiler_params=pltpu.CompilerParams(vmem_limit_bytes=24 * 2**20),
    )(*operands)


def stages(records, pattern, iterate):
    place = jnp.stack([lax.axis_index("row"), lax.axis_index("col")]).astype(jnp.int32)
    tile = jax.ShapeDtypeStruct((BLOCK, 2 * BLOCK), jnp.float32)
    stored = HBM((NB * BLOCK, 2 * BLOCK), jnp.bfloat16)
    tiles = HBM((16, BLOCK, 2 * BLOCK), jnp.float32)
    iterate_col = lax.all_gather(iterate, "row", axis=0, tiled=True)
    cores = [[2 * z + core for z in range(16)] for core in range(2)]
    partner = [(r, r ^ 1) for r in range(NB)]
    left = VMEM((2, FIELDS, BLOCK, BLOCK), jnp.float32)
    square = VMEM((BLOCK, BLOCK), jnp.float32)
    table = VMEM((FIELDS, NB, BLOCK), jnp.float32)
    both = jnp.stack([records, lax.ppermute(records, "row", partner)])
    everyone = lax.all_gather(both, "row", axis=0, axis_index_groups=cores)
    sems = pltpu.SemaphoreType.DMA((16,))
    wide = VMEM((2 * BLOCK, NB * BLOCK), jnp.bfloat16)
    copies = call(hbm_copies_kernel, tiles, [sems], iterate, outs=(HBM,), scalars=0)
    iterate_row = exchange(copies, "col")
    fields, product_one = call(
        first_kernel,
        (table, tiles),
        [left, square, wide, wide, VMEM((BLOCK, 2 * BLOCK), jnp.float32), sems],
        place,
        pattern,
        everyone,
        iterate_row,
        on_chip=(2, 3),
        outs=(VMEM, HBM),
    )
    margin = call(margin_kernel, tile, [left, square], place, pattern, fields, on_chip=(2,))
    one_row = exchange(product_one, "col")
    window = (PANEL, 2 * BLOCK)
    high, low = call(
        prepare_kernel,
        (stored, stored),
        [],
        place,
        pattern,
        iterate_col,
        outs=(window, window),
        grid=(NB * BLOCK // PANEL,),
        blocks={2: window},
        stay=(2,),
    )
    half = VMEM((16, 8, BLOCK), jnp.float32)
    turned = VMEM((2, BLOCK, BLOCK), jnp.float32)
    window = (PART, 2 * BLOCK)
    kept, given = call(
        second_kernel,
        (half, half),
        [VMEM((BLOCK, 2 * BLOCK), jnp.float32), turned],
        place,
        pattern,
        one_row,
        high,
        low,
        on_chip=(2,),
        grid=(NB * BLOCK // PART,),
        blocks={3: window, 4: window},
        stay=(3, 4),
    )
    given = lax.ppermute(given, "row", partner)
    slices = jnp.stack([kept, given], axis=1)
    slices = exchange(slices, "col")
    slices = lax.all_to_all(slices, "row", 0, 0, tiled=True, axis_index_groups=cores)
    copies = VMEM((16,) + slices.shape, jnp.float32)
    slices = call(replicate_kernel, copies, [], slices, on_chip=(0,), scalars=0)
    two_row = exchange(slices, "col")
    updated = call(third_kernel, tile, [], place, pattern, two_row, high, low, iterate, on_chip=(2, 3, 4))
    return (margin, updated)


def solution(mesh):
    in_specs = (P(None, "row"), P(), P("row", "col"))
    out_specs = (P("row", "col"), P("row", "col"))
    return jax.shard_map(stages, mesh=mesh, in_specs=in_specs, out_specs=out_specs, check_vma=False)
```

```python
import jax
import jax.numpy as jnp
from jax import lax
from jax.experimental import pallas as pl
from jax.experimental.pallas import tpu as pltpu
from jax.sharding import PartitionSpec as P


BLOCK = 128
PRIMS = 3
NB = 32
FIELDS = 3 + 2 * PRIMS
CHUNK = 128
PANEL = 1024
PART = 1024
ROOMS = (24,)
LOG2E = 1.4426950408889634
VMEM = pltpu.VMEM
SMEM = pltpu.SMEM
HBM = pltpu.HBM


def split(value):
    high = value.astype(jnp.bfloat16)
    low = (value - high.astype(jnp.float32)).astype(jnp.bfloat16)
    return high, low


def dot_transposed(left, right):
    return lax.dot_general(left, right, (((1,), (1,)), ((), ())), preferred_element_type=jnp.float32)


def half_tile(fields_ref, left_ref, tile_ref, half, block):
    right = [fields_ref[f, pl.ds(block, 1), :] for f in range(FIELDS)]

    def chunk(step, carry):
        rows = pl.ds(pl.multiple_of(step * CHUNK, CHUNK), CHUNK)
        left = [left_ref[half, f, rows, :] for f in range(FIELDS)]
        distance = (left[0] - right[0]) ** 2
        distance = distance + (left[1] - right[1]) ** 2
        distance = (distance + (left[2] - right[2]) ** 2) * -LOG2E
        total = jnp.zeros_like(distance)
        for p in range(PRIMS):
            stretched = left[3 + p] * distance
            for q in range(PRIMS):
                inverse_root = lax.rsqrt(left[3 + p] + right[3 + q])
                root = (left[6 + p] * inverse_root) * right[6 + q]
                decay = jnp.exp2((stretched * (inverse_root * inverse_root)) * right[3 + q])
                total = total + ((root * root) * root) * decay
        tile_ref[rows, :] = total
        return carry

    lax.fori_loop(0, BLOCK // CHUNK, chunk, 0)


def slot(core, block):
    return (core ^ (block % 2)) * (NB // 2) + block // 2


def spread_own(fields, left, core, col):
    for half in range(2):
        for f in range(FIELDS):
            own = fields[f, pl.ds(slot(core, 2 * col + half), 1), :]
            left[half, f] = jnp.broadcast_to(own, (BLOCK, BLOCK)).T


def send_copies(tile, copies, sems):
    moves = [pltpu.make_async_copy(tile, copies.at[k], sems.at[k]) for k in range(16)]
    for move in moves:
        move.start()
    for move in moves:
        move.wait()


def first_kernel(place, pattern, records, iterate_row, fields, copies, left, tile, high, low, one, sems):
    row, col = place[0], place[1]
    core = row % 2
    for part in range(2):
        half_table = slice(part * NB // 2, (part + 1) * NB // 2)
        exponents = [records[:, part, 3 + p, :] for p in range(PRIMS)]
        coefficients = [records[:, part, 3 + PRIMS + p, :] for p in range(PRIMS)]
        roots = [jnp.sqrt(e) for e in exponents]
        norm = jnp.zeros_like(exponents[0])
        for p in range(PRIMS):
            for q in range(PRIMS):
                ratio = 2.0 * roots[p] * roots[q] / (exponents[p] + exponents[q])
                norm = norm + coefficients[p] * coefficients[q] * (ratio * jnp.sqrt(ratio))
        scale = (2.0**0.75) * lax.rsqrt(norm)
        for f in range(3):
            fields[f, half_table] = records[:, part, f, :]
        for p in range(PRIMS):
            weight = jnp.exp2(jnp.log2(coefficients[p] * scale) * (1.0 / 3.0))
            fields[3 + p, half_table] = exponents[p]
            fields[6 + p, half_table] = weight * jnp.sqrt(roots[p])
    spread_own(fields, left, core, col)

    def step(index, carry):
        half, block = index // NB, index % NB
        own = 2 * col + half
        needed = pattern[own, block] * pattern[block, row] * pattern[row, own]
        rows = pl.ds(pl.multiple_of(block * BLOCK, BLOCK), BLOCK)
        lanes = pl.ds(pl.multiple_of(half * BLOCK, BLOCK), BLOCK)

        @pl.when(needed != 0)
        def _():
            half_tile(fields, left, tile, half, slot(core, block))
            high[lanes, rows], low[lanes, rows] = split(tile[...])

        @pl.when(needed == 0)
        def _():
            high[lanes, rows] = jnp.zeros((BLOCK, BLOCK), jnp.bfloat16)
            low[lanes, rows] = jnp.zeros((BLOCK, BLOCK), jnp.bfloat16)

        return carry

    lax.fori_loop(0, 2 * NB, step, 0)
    total = jnp.zeros((BLOCK, 2 * BLOCK), jnp.float32)
    for k in range(16):
        columns = slice(2 * BLOCK * k, 2 * BLOCK * (k + 1))
        piece_high, piece_low = split(iterate_row[k])
        total = total + dot_transposed(piece_high, high[:, columns])
        total = total + dot_transposed(piece_high, low[:, columns])
        total = total + dot_transposed(piece_low, high[:, columns])
    one[...] = total
    send_copies(one, copies, sems)


def margin_kernel(place, pattern, fields, margin, left, tile):
    row, col = place[0], place[1]
    spread_own(fields, left, row % 2, col)
    for half in range(2):
        margin_live = pattern[row, 2 * col + half] != 0
        lanes = slice(half * BLOCK, (half + 1) * BLOCK)

        @pl.when(margin_live)
        def _():
            half_tile(fields, left, tile, half, slot(row % 2, row))
            margin[:, lanes] = tile[...].T

        @pl.when(jnp.logical_not(margin_live))
        def _():
            margin[:, lanes] = jnp.zeros((BLOCK, BLOCK), jnp.float32)


def hbm_copies_kernel(value, copies, sems):
    send_copies(value, copies, sems)


def list_live(pattern, row, order):
    for k in range(NB):
        order[k] = 0

    def step(k, count):
        @pl.when(pattern[row, k] != 0)
        def _():
            order[count] = k

        return count + (pattern[row, k] != 0).astype(jnp.int32)

    return lax.fori_loop(0, NB, step, jnp.int32(0))


def compact_kernel(place, pattern, slices, copies, order, line):
    row = place[0]
    core = row % 2
    count = list_live(pattern, row, order)
    for i in range(line.shape[0]):
        kept = (i < count).astype(jnp.float32)
        line[i] = kept * slices[order[i] // 2, core ^ (order[i] % 2)]
    for copy in range(16):
        copies[copy] = line[...]


def prepare_kernel(place, pattern, iterate_col, high, low):
    col = place[1]
    first = pl.program_id(0) * (PANEL // BLOCK)
    for block in range(PANEL // BLOCK):
        rows = slice(block * BLOCK, (block + 1) * BLOCK)
        for half in range(2):
            lanes = slice(half * BLOCK, (half + 1) * BLOCK)
            mask = live(pattern, first + block, 2 * col + half)
            high[rows, lanes], low[rows, lanes] = split(mask * iterate_col[rows, lanes])


def contract(pieces, high, low):
    total = jnp.zeros((BLOCK, 2 * BLOCK), jnp.float32)
    for k, piece in enumerate(pieces):
        rows = slice(2 * BLOCK * k, 2 * BLOCK * (k + 1))
        piece_high, piece_low = split(piece)
        total = total + jnp.dot(piece_high, high[rows], preferred_element_type=jnp.float32)
        total = total + jnp.dot(piece_high, low[rows], preferred_element_type=jnp.float32)
        total = total + jnp.dot(piece_low, high[rows], preferred_element_type=jnp.float32)
    return total


def live(pattern, row, column):
    return (pattern[row, column] != 0).astype(jnp.float32)


def second_kernel(place, pattern, one_row, high, low, kept, given, total, tile):
    row, col = place[0], place[1]
    part = pl.program_id(0)
    pieces = PART // (2 * BLOCK)
    product = contract([one_row[k] for k in range(pieces)], high, low)

    @pl.when(part == 0)
    def _():
        total[...] = product

    @pl.when(part > 0)
    def _():
        total[...] += product

    @pl.when(part == pl.num_programs(0) - 1)
    def _():
        for half in range(2):
            own = total[:, half * BLOCK : (half + 1) * BLOCK]
            tile[half] = (live(pattern, row, 2 * col + half) * own).T
        core = row % 2
        kept[...] = tile[core].reshape(BLOCK // 8, 8, BLOCK)
        given[...] = tile[1 - core].reshape(BLOCK // 8, 8, BLOCK)


def third_kernel(place, pattern, two_row, high, low, iterate, updated, order):
    row, col = place[0], place[1]
    list_live(pattern, row, order)
    total = jnp.zeros((BLOCK, 2 * BLOCK), jnp.float32)
    for i in range(0, two_row.shape[1], 2):
        pair = [two_row[:, i + h].reshape(BLOCK, BLOCK) for h in range(2)]
        rows = [pl.ds(pl.multiple_of(order[i + h] * BLOCK, BLOCK), BLOCK) for h in range(2)]
        piece_high, piece_low = split(jnp.concatenate(pair, axis=1))
        part_high = jnp.concatenate([high[r, :] for r in rows], axis=0)
        part_low = jnp.concatenate([low[r, :] for r in rows], axis=0)
        total = total + jnp.dot(piece_high, part_high, preferred_element_type=jnp.float32)
        total = total + jnp.dot(piece_high, part_low, preferred_element_type=jnp.float32)
        total = total + jnp.dot(piece_low, part_high, preferred_element_type=jnp.float32)
    for half in range(2):
        lanes = slice(half * BLOCK, (half + 1) * BLOCK)
        mask = live(pattern, row, 2 * col + half)
        updated[:, lanes] = mask * (1.5 * iterate[:, lanes] - 0.5 * total[:, lanes])


def exchange(pieces, axis):
    return lax.all_to_all(pieces, axis, 0, 0, tiled=True)


def call(kernel, out_shapes, scratch, *operands, on_chip=(), outs=None, scalars=2, grid=(), blocks=None, stay=()):
    whole = pl.BlockSpec(memory_space=VMEM)
    in_specs = [pl.BlockSpec(memory_space=SMEM)] * scalars + [whole] * (len(operands) - scalars)
    blocks = blocks or {}
    for k, block in blocks.items():
        if k < len(operands):
            in_specs[k] = pl.BlockSpec(block, lambda i, rest=len(block) - 1: (i,) + (0,) * rest)
    operands = list(operands)
    for k in on_chip:
        operands[k] = pltpu.with_memory_space_constraint(operands[k], VMEM)
    for k in stay:
        operands[k] = pltpu.with_memory_space_constraint(operands[k], HBM)
    if outs is None:
        out_specs = jax.tree.map(lambda _: whole, out_shapes)
    else:
        out_specs = tuple(
            pl.BlockSpec(space, lambda i: (i, 0)) if isinstance(space, tuple) else pl.BlockSpec(memory_space=space)
            for space in outs
        )
        out_specs = out_specs if isinstance(out_shapes, tuple) else out_specs[0]
    return pl.pallas_call(
        kernel,
        out_shape=out_shapes,
        grid=grid,
        in_specs=in_specs,
        out_specs=out_specs,
        scratch_shapes=scratch,
        compiler_params=pltpu.CompilerParams(vmem_limit_bytes=24 * 2**20),
    )(*operands)


def stages(records, pattern, iterate):
    place = jnp.stack([lax.axis_index("row"), lax.axis_index("col")]).astype(jnp.int32)
    fullest = jnp.max(jnp.sum((pattern != 0).astype(jnp.int32), axis=1))
    place, roomy = lax.optimization_barrier((place, fullest > ROOMS[0]))
    tile = jax.ShapeDtypeStruct((BLOCK, 2 * BLOCK), jnp.float32)
    stored = HBM((NB * BLOCK, 2 * BLOCK), jnp.bfloat16)
    tiles = HBM((16, BLOCK, 2 * BLOCK), jnp.float32)
    iterate_col = lax.all_gather(iterate, "row", axis=0, tiled=True)
    cores = [[2 * z + core for z in range(16)] for core in range(2)]
    partner = [(r, r ^ 1) for r in range(NB)]
    left = VMEM((2, FIELDS, BLOCK, BLOCK), jnp.float32)
    square = VMEM((BLOCK, BLOCK), jnp.float32)
    table = VMEM((FIELDS, NB, BLOCK), jnp.float32)
    both = jnp.stack([records, lax.ppermute(records, "row", partner)])
    everyone = lax.all_gather(both, "row", axis=0, axis_index_groups=cores)
    sems = pltpu.SemaphoreType.DMA((16,))
    wide = VMEM((2 * BLOCK, NB * BLOCK), jnp.bfloat16)
    copies = call(hbm_copies_kernel, tiles, [sems], iterate, outs=(HBM,), scalars=0)
    iterate_row = exchange(copies, "col")
    fields, product_one = call(
        first_kernel,
        (table, tiles),
        [left, square, wide, wide, VMEM((BLOCK, 2 * BLOCK), jnp.float32), sems],
        place,
        pattern,
        everyone,
        iterate_row,
        on_chip=(2, 3),
        outs=(VMEM, HBM),
    )
    margin = call(margin_kernel, tile, [left, square], place, pattern, fields, on_chip=(2,))
    one_row = exchange(product_one, "col")
    window = (PANEL, 2 * BLOCK)
    high, low = call(
        prepare_kernel,
        (stored, stored),
        [],
        place,
        pattern,
        iterate_col,
        outs=(window, window),
        grid=(NB * BLOCK // PANEL,),
        blocks={2: window},
        stay=(2,),
    )
    half = VMEM((16, 8, BLOCK), jnp.float32)
    turned = VMEM((2, BLOCK, BLOCK), jnp.float32)
    window = (PART, 2 * BLOCK)
    kept, given = call(
        second_kernel,
        (half, half),
        [VMEM((BLOCK, 2 * BLOCK), jnp.float32), turned],
        place,
        pattern,
        one_row,
        high,
        low,
        grid=(NB * BLOCK // PART,),
        blocks={2: (PART // (2 * BLOCK), BLOCK, 2 * BLOCK), 3: window, 4: window},
        stay=(2, 3, 4),
    )
    given = lax.ppermute(given, "row", partner)
    slices = jnp.stack([kept, given], axis=1)
    slices = exchange(slices, "col")
    slices = lax.all_to_all(slices, "row", 0, 0, tiled=True, axis_index_groups=cores)
    order = SMEM((NB,), jnp.int32)

    def finish(room):
        def branch(place, pattern, slices, high, low, iterate):
            line = VMEM((room, 8, BLOCK), jnp.float32)
            copies = VMEM((16, room, 8, BLOCK), jnp.float32)
            copies = call(compact_kernel, copies, [order, line], place, pattern, slices, on_chip=(2,))
            two_row = exchange(copies, "col")
            return call(
                third_kernel, tile, [order], place, pattern, two_row, high, low, iterate, on_chip=(2, 3, 4)
            )

        return branch

    slices, roomy = lax.optimization_barrier((slices, roomy))
    updated = lax.cond(roomy, finish(NB), finish(ROOMS[0]), place, pattern, slices, high, low, iterate)
    return (margin, updated)


def solution(mesh):
    in_specs = (P(None, "row"), P(), P("row", "col"))
    out_specs = (P("row", "col"), P("row", "col"))
    return jax.shard_map(stages, mesh=mesh, in_specs=in_specs, out_specs=out_specs, check_vma=False)
```

```python
import jax
import jax.numpy as jnp
from jax import lax
from jax.experimental import pallas as pl
from jax.experimental.pallas import tpu as pltpu
from jax.sharding import PartitionSpec as P


BLOCK = 128
PRIMS = 3
NB = 32
FIELDS = 3 + 2 * PRIMS
CHUNK = 128
PANEL = 1024
PART = 1024
ROOMS = (20, 24, 28, NB)
LOG2E = 1.4426950408889634
VMEM = pltpu.VMEM
SMEM = pltpu.SMEM
HBM = pltpu.HBM


def split(value):
    high = value.astype(jnp.bfloat16)
    low = (value - high.astype(jnp.float32)).astype(jnp.bfloat16)
    return high, low


def dot_transposed(left, right):
    return lax.dot_general(left, right, (((1,), (1,)), ((), ())), preferred_element_type=jnp.float32)


def half_tile(fields_ref, left_ref, tile_ref, half, block):
    right = [fields_ref[f, pl.ds(block, 1), :] for f in range(FIELDS)]

    def chunk(step, carry):
        rows = pl.ds(pl.multiple_of(step * CHUNK, CHUNK), CHUNK)
        left = [left_ref[half, f, rows, :] for f in range(FIELDS)]
        distance = (left[0] - right[0]) ** 2
        distance = distance + (left[1] - right[1]) ** 2
        distance = (distance + (left[2] - right[2]) ** 2) * -LOG2E
        total = jnp.zeros_like(distance)
        for p in range(PRIMS):
            stretched = left[3 + p] * distance
            for q in range(PRIMS):
                inverse_root = lax.rsqrt(left[3 + p] + right[3 + q])
                root = (left[6 + p] * inverse_root) * right[6 + q]
                decay = jnp.exp2((stretched * (inverse_root * inverse_root)) * right[3 + q])
                total = total + ((root * root) * root) * decay
        tile_ref[rows, :] = total
        return carry

    lax.fori_loop(0, BLOCK // CHUNK, chunk, 0)


def slot(core, block):
    return (core ^ (block % 2)) * (NB // 2) + block // 2


def spread_own(fields, left, core, col):
    for half in range(2):
        for f in range(FIELDS):
            own = fields[f, pl.ds(slot(core, 2 * col + half), 1), :]
            left[half, f] = jnp.broadcast_to(own, (BLOCK, BLOCK)).T


def send_copies(tile, copies, sems):
    moves = [pltpu.make_async_copy(tile, copies.at[k], sems.at[k]) for k in range(16)]
    for move in moves:
        move.start()
    for move in moves:
        move.wait()


def first_kernel(place, pattern, records, iterate_row, fields, copies, left, tile, high, low, one, sems):
    row, col = place[0], place[1]
    core = row % 2
    for part in range(2):
        half_table = slice(part * NB // 2, (part + 1) * NB // 2)
        exponents = [records[:, part, 3 + p, :] for p in range(PRIMS)]
        coefficients = [records[:, part, 3 + PRIMS + p, :] for p in range(PRIMS)]
        roots = [jnp.sqrt(e) for e in exponents]
        norm = jnp.zeros_like(exponents[0])
        for p in range(PRIMS):
            for q in range(PRIMS):
                ratio = 2.0 * roots[p] * roots[q] / (exponents[p] + exponents[q])
                norm = norm + coefficients[p] * coefficients[q] * (ratio * jnp.sqrt(ratio))
        scale = (2.0**0.75) * lax.rsqrt(norm)
        for f in range(3):
            fields[f, half_table] = records[:, part, f, :]
        for p in range(PRIMS):
            weight = jnp.exp2(jnp.log2(coefficients[p] * scale) * (1.0 / 3.0))
            fields[3 + p, half_table] = exponents[p]
            fields[6 + p, half_table] = weight * jnp.sqrt(roots[p])
    spread_own(fields, left, core, col)

    def step(index, carry):
        half, block = index // NB, index % NB
        own = 2 * col + half
        needed = pattern[own, block] * pattern[block, row] * pattern[row, own]
        rows = pl.ds(pl.multiple_of(block * BLOCK, BLOCK), BLOCK)
        lanes = pl.ds(pl.multiple_of(half * BLOCK, BLOCK), BLOCK)

        @pl.when(needed != 0)
        def _():
            half_tile(fields, left, tile, half, slot(core, block))
            high[lanes, rows], low[lanes, rows] = split(tile[...])

        @pl.when(needed == 0)
        def _():
            high[lanes, rows] = jnp.zeros((BLOCK, BLOCK), jnp.bfloat16)
            low[lanes, rows] = jnp.zeros((BLOCK, BLOCK), jnp.bfloat16)

        return carry

    lax.fori_loop(0, 2 * NB, step, 0)
    total = jnp.zeros((BLOCK, 2 * BLOCK), jnp.float32)
    for k in range(16):
        columns = slice(2 * BLOCK * k, 2 * BLOCK * (k + 1))
        piece_high, piece_low = split(iterate_row[k])
        total = total + dot_transposed(piece_high, high[:, columns])
        total = total + dot_transposed(piece_high, low[:, columns])
        total = total + dot_transposed(piece_low, high[:, columns])
    one[...] = total
    send_copies(one, copies, sems)


def margin_kernel(place, pattern, fields, margin, left, tile):
    row, col = place[0], place[1]
    spread_own(fields, left, row % 2, col)
    for half in range(2):
        margin_live = pattern[row, 2 * col + half] != 0
        lanes = slice(half * BLOCK, (half + 1) * BLOCK)

        @pl.when(margin_live)
        def _():
            half_tile(fields, left, tile, half, slot(row % 2, row))
            margin[:, lanes] = tile[...].T

        @pl.when(jnp.logical_not(margin_live))
        def _():
            margin[:, lanes] = jnp.zeros((BLOCK, BLOCK), jnp.float32)


def hbm_copies_kernel(value, copies, sems):
    send_copies(value, copies, sems)


def list_live(pattern, row, order):
    for k in range(NB):
        order[k] = 0

    def step(k, count):
        @pl.when(pattern[row, k] != 0)
        def _():
            order[count] = k

        return count + (pattern[row, k] != 0).astype(jnp.int32)

    return lax.fori_loop(0, NB, step, jnp.int32(0))


def compact_kernel(place, pattern, slices, copies, order, line):
    row = place[0]
    core = row % 2
    count = list_live(pattern, row, order)
    for i in range(line.shape[0]):
        kept = (i < count).astype(jnp.float32)
        line[i] = kept * slices[order[i] // 2, core ^ (order[i] % 2)]
    for copy in range(16):
        copies[copy] = line[...]


def prepare_kernel(place, pattern, iterate_col, high, low):
    col = place[1]
    first = pl.program_id(0) * (PANEL // BLOCK)
    for block in range(PANEL // BLOCK):
        rows = slice(block * BLOCK, (block + 1) * BLOCK)
        for half in range(2):
            lanes = slice(half * BLOCK, (half + 1) * BLOCK)
            mask = live(pattern, first + block, 2 * col + half)
            high[rows, lanes], low[rows, lanes] = split(mask * iterate_col[rows, lanes])


def contract(pieces, high, low):
    total = jnp.zeros((BLOCK, 2 * BLOCK), jnp.float32)
    for k, piece in enumerate(pieces):
        rows = slice(2 * BLOCK * k, 2 * BLOCK * (k + 1))
        piece_high, piece_low = split(piece)
        total = total + jnp.dot(piece_high, high[rows], preferred_element_type=jnp.float32)
        total = total + jnp.dot(piece_high, low[rows], preferred_element_type=jnp.float32)
        total = total + jnp.dot(piece_low, high[rows], preferred_element_type=jnp.float32)
    return total


def live(pattern, row, column):
    return (pattern[row, column] != 0).astype(jnp.float32)


def second_kernel(place, pattern, one_row, high, low, kept, given, total, tile):
    row, col = place[0], place[1]
    part = pl.program_id(0)
    pieces = PART // (2 * BLOCK)
    product = contract([one_row[k] for k in range(pieces)], high, low)

    @pl.when(part == 0)
    def _():
        total[...] = product

    @pl.when(part > 0)
    def _():
        total[...] += product

    @pl.when(part == pl.num_programs(0) - 1)
    def _():
        for half in range(2):
            own = total[:, half * BLOCK : (half + 1) * BLOCK]
            tile[half] = (live(pattern, row, 2 * col + half) * own).T
        core = row % 2
        kept[...] = tile[core].reshape(BLOCK // 8, 8, BLOCK)
        given[...] = tile[1 - core].reshape(BLOCK // 8, 8, BLOCK)


def third_kernel(place, pattern, two_row, high, low, iterate, updated, order):
    row, col = place[0], place[1]
    list_live(pattern, row, order)
    total = jnp.zeros((BLOCK, 2 * BLOCK), jnp.float32)
    for i in range(0, two_row.shape[1], 2):
        pair = [two_row[:, i + h].reshape(BLOCK, BLOCK) for h in range(2)]
        rows = [pl.ds(pl.multiple_of(order[i + h] * BLOCK, BLOCK), BLOCK) for h in range(2)]
        piece_high, piece_low = split(jnp.concatenate(pair, axis=1))
        part_high = jnp.concatenate([high[r, :] for r in rows], axis=0)
        part_low = jnp.concatenate([low[r, :] for r in rows], axis=0)
        total = total + jnp.dot(piece_high, part_high, preferred_element_type=jnp.float32)
        total = total + jnp.dot(piece_high, part_low, preferred_element_type=jnp.float32)
        total = total + jnp.dot(piece_low, part_high, preferred_element_type=jnp.float32)
    for half in range(2):
        lanes = slice(half * BLOCK, (half + 1) * BLOCK)
        mask = live(pattern, row, 2 * col + half)
        updated[:, lanes] = mask * (1.5 * iterate[:, lanes] - 0.5 * total[:, lanes])


def exchange(pieces, axis):
    return lax.all_to_all(pieces, axis, 0, 0, tiled=True)


def call(kernel, out_shapes, scratch, *operands, on_chip=(), outs=None, scalars=2, grid=(), blocks=None, stay=()):
    whole = pl.BlockSpec(memory_space=VMEM)
    in_specs = [pl.BlockSpec(memory_space=SMEM)] * scalars + [whole] * (len(operands) - scalars)
    blocks = blocks or {}
    for k, block in blocks.items():
        if k < len(operands):
            in_specs[k] = pl.BlockSpec(block, lambda i, rest=len(block) - 1: (i,) + (0,) * rest)
    operands = list(operands)
    for k in on_chip:
        operands[k] = pltpu.with_memory_space_constraint(operands[k], VMEM)
    for k in stay:
        operands[k] = pltpu.with_memory_space_constraint(operands[k], HBM)
    if outs is None:
        out_specs = jax.tree.map(lambda _: whole, out_shapes)
    else:
        out_specs = tuple(
            pl.BlockSpec(space, lambda i: (i, 0)) if isinstance(space, tuple) else pl.BlockSpec(memory_space=space)
            for space in outs
        )
        out_specs = out_specs if isinstance(out_shapes, tuple) else out_specs[0]
    return pl.pallas_call(
        kernel,
        out_shape=out_shapes,
        grid=grid,
        in_specs=in_specs,
        out_specs=out_specs,
        scratch_shapes=scratch,
        compiler_params=pltpu.CompilerParams(vmem_limit_bytes=24 * 2**20),
    )(*operands)


def stages(records, pattern, iterate):
    place = jnp.stack([lax.axis_index("row"), lax.axis_index("col")]).astype(jnp.int32)
    fullest = jnp.max(jnp.sum((pattern != 0).astype(jnp.int32), axis=1))
    choice = sum((fullest > room).astype(jnp.int32) for room in ROOMS[:-1])
    place, choice = lax.optimization_barrier((place, choice))
    tile = jax.ShapeDtypeStruct((BLOCK, 2 * BLOCK), jnp.float32)
    stored = HBM((NB * BLOCK, 2 * BLOCK), jnp.bfloat16)
    tiles = HBM((16, BLOCK, 2 * BLOCK), jnp.float32)
    iterate_col = lax.all_gather(iterate, "row", axis=0, tiled=True)
    cores = [[2 * z + core for z in range(16)] for core in range(2)]
    partner = [(r, r ^ 1) for r in range(NB)]
    left = VMEM((2, FIELDS, BLOCK, BLOCK), jnp.float32)
    square = VMEM((BLOCK, BLOCK), jnp.float32)
    table = VMEM((FIELDS, NB, BLOCK), jnp.float32)
    both = jnp.stack([records, lax.ppermute(records, "row", partner)])
    everyone = lax.all_gather(both, "row", axis=0, axis_index_groups=cores)
    sems = pltpu.SemaphoreType.DMA((16,))
    wide = VMEM((2 * BLOCK, NB * BLOCK), jnp.bfloat16)
    copies = call(hbm_copies_kernel, tiles, [sems], iterate, outs=(HBM,), scalars=0)
    iterate_row = exchange(copies, "col")
    fields, product_one = call(
        first_kernel,
        (table, tiles),
        [left, square, wide, wide, VMEM((BLOCK, 2 * BLOCK), jnp.float32), sems],
        place,
        pattern,
        everyone,
        iterate_row,
        on_chip=(2, 3),
        outs=(VMEM, HBM),
    )
    margin = call(margin_kernel, tile, [left, square], place, pattern, fields, on_chip=(2,))
    one_row = exchange(product_one, "col")
    window = (PANEL, 2 * BLOCK)
    high, low = call(
        prepare_kernel,
        (stored, stored),
        [],
        place,
        pattern,
        iterate_col,
        outs=(window, window),
        grid=(NB * BLOCK // PANEL,),
        blocks={2: window},
        stay=(2,),
    )
    half = VMEM((16, 8, BLOCK), jnp.float32)
    turned = VMEM((2, BLOCK, BLOCK), jnp.float32)
    window = (PART, 2 * BLOCK)
    kept, given = call(
        second_kernel,
        (half, half),
        [VMEM((BLOCK, 2 * BLOCK), jnp.float32), turned],
        place,
        pattern,
        one_row,
        high,
        low,
        grid=(NB * BLOCK // PART,),
        blocks={2: (PART // (2 * BLOCK), BLOCK, 2 * BLOCK), 3: window, 4: window},
        stay=(2, 3, 4),
    )
    given = lax.ppermute(given, "row", partner)
    slices = jnp.stack([kept, given], axis=1)
    slices = exchange(slices, "col")
    slices = lax.all_to_all(slices, "row", 0, 0, tiled=True, axis_index_groups=cores)
    order = SMEM((NB,), jnp.int32)

    def finish(room):
        def branch(place, pattern, slices, high, low, iterate):
            line = VMEM((room, 8, BLOCK), jnp.float32)
            copies = VMEM((16, room, 8, BLOCK), jnp.float32)
            copies = call(compact_kernel, copies, [order, line], place, pattern, slices, on_chip=(2,))
            two_row = exchange(copies, "col")
            return call(
                third_kernel, tile, [order], place, pattern, two_row, high, low, iterate, on_chip=(2, 3, 4)
            )

        return branch

    slices, choice = lax.optimization_barrier((slices, choice))
    branches = [finish(room) for room in ROOMS]
    updated = lax.switch(choice, branches, place, pattern, slices, high, low, iterate)
    return (margin, updated)


def solution(mesh):
    in_specs = (P(None, "row"), P(), P("row", "col"))
    out_specs = (P("row", "col"), P("row", "col"))
    return jax.shard_map(stages, mesh=mesh, in_specs=in_specs, out_specs=out_specs, check_vma=False)
```

```python
import jax
import jax.numpy as jnp
from jax import lax
from jax.experimental import pallas as pl
from jax.experimental.pallas import tpu as pltpu
from jax.sharding import PartitionSpec as P


BLOCK = 128
PRIMS = 3
NB = 32
FIELDS = 3 + 2 * PRIMS
CHUNK = 128
PANEL = 1024
PART = 1024
ROOMS = (20, 24, 28, NB)
LOG2E = 1.4426950408889634
VMEM = pltpu.VMEM
SMEM = pltpu.SMEM
HBM = pltpu.HBM


def split(value):
    high = value.astype(jnp.bfloat16)
    low = (value - high.astype(jnp.float32)).astype(jnp.bfloat16)
    return high, low


def dot_transposed(left, right):
    return lax.dot_general(left, right, (((1,), (1,)), ((), ())), preferred_element_type=jnp.float32)


def half_tile(fields_ref, left_ref, tile_ref, half, core, block):
    right = [row_of(fields_ref, core, block, f) for f in range(FIELDS)]

    def chunk(step, carry):
        rows = pl.ds(pl.multiple_of(step * CHUNK, CHUNK), CHUNK)
        left = [left_ref[half, f, rows, :] for f in range(FIELDS)]
        distance = (left[0] - right[0]) ** 2
        distance = distance + (left[1] - right[1]) ** 2
        distance = (distance + (left[2] - right[2]) ** 2) * -LOG2E
        total = jnp.zeros_like(distance)
        for p in range(PRIMS):
            stretched = left[3 + p] * distance
            for q in range(PRIMS):
                inverse_root = lax.rsqrt(left[3 + p] + right[3 + q])
                root = (left[6 + p] * inverse_root) * right[6 + q]
                decay = jnp.exp2((stretched * (inverse_root * inverse_root)) * right[3 + q])
                total = total + ((root * root) * root) * decay
        tile_ref[rows, :] = total
        return carry

    lax.fori_loop(0, BLOCK // CHUNK, chunk, 0)


def row_of(fields, core, block, f):
    return fields[block // 2, core ^ (block % 2), f : f + 1, :]


def spread_own(fields, left, core, col):
    for half in range(2):
        for f in range(FIELDS):
            own = row_of(fields, core, 2 * col + half, f)
            left[half, f] = jnp.broadcast_to(own, (BLOCK, BLOCK)).T


def send_copies(tile, copies, sems):
    moves = [pltpu.make_async_copy(tile, copies.at[k], sems.at[k]) for k in range(16)]
    for move in moves:
        move.start()
    for move in moves:
        move.wait()


def first_kernel(place, pattern, fields, iterate_row, copies, left, tile, high, low, one, sems):
    row, col = place[0], place[1]
    core = row % 2
    spread_own(fields, left, core, col)

    def step(index, carry):
        half, block = index // NB, index % NB
        own = 2 * col + half
        needed = pattern[own, block] * pattern[block, row] * pattern[row, own]
        rows = pl.ds(pl.multiple_of(block * BLOCK, BLOCK), BLOCK)
        lanes = pl.ds(pl.multiple_of(half * BLOCK, BLOCK), BLOCK)

        @pl.when(needed != 0)
        def _():
            half_tile(fields, left, tile, half, core, block)
            high[lanes, rows], low[lanes, rows] = split(tile[...])

        @pl.when(needed == 0)
        def _():
            high[lanes, rows] = jnp.zeros((BLOCK, BLOCK), jnp.bfloat16)
            low[lanes, rows] = jnp.zeros((BLOCK, BLOCK), jnp.bfloat16)

        return carry

    lax.fori_loop(0, 2 * NB, step, 0)
    total = jnp.zeros((BLOCK, 2 * BLOCK), jnp.float32)
    for k in range(16):
        columns = slice(2 * BLOCK * k, 2 * BLOCK * (k + 1))
        piece_high, piece_low = split(iterate_row[k])
        total = total + dot_transposed(piece_high, high[:, columns])
        total = total + dot_transposed(piece_high, low[:, columns])
        total = total + dot_transposed(piece_low, high[:, columns])
    one[...] = total
    send_copies(one, copies, sems)


def margin_kernel(place, pattern, fields, margin, left, tile):
    row, col = place[0], place[1]
    spread_own(fields, left, row % 2, col)
    for half in range(2):
        margin_live = pattern[row, 2 * col + half] != 0
        lanes = slice(half * BLOCK, (half + 1) * BLOCK)

        @pl.when(margin_live)
        def _():
            half_tile(fields, left, tile, half, row % 2, row)
            margin[:, lanes] = tile[...].T

        @pl.when(jnp.logical_not(margin_live))
        def _():
            margin[:, lanes] = jnp.zeros((BLOCK, BLOCK), jnp.float32)


def start_kernel(records, value, fields, copies, sems):
    moves = [pltpu.make_async_copy(value, copies.at[k], sems.at[k]) for k in range(16)]
    for move in moves:
        move.start()
    exponents = [records[3 + p : 4 + p, :] for p in range(PRIMS)]
    coefficients = [records[3 + PRIMS + p : 4 + PRIMS + p, :] for p in range(PRIMS)]
    roots = [jnp.sqrt(e) for e in exponents]
    norm = jnp.zeros_like(exponents[0])
    for p in range(PRIMS):
        for q in range(PRIMS):
            ratio = 2.0 * roots[p] * roots[q] / (exponents[p] + exponents[q])
            norm = norm + coefficients[p] * coefficients[q] * (ratio * jnp.sqrt(ratio))
    scale = (2.0**0.75) * lax.rsqrt(norm)
    fields[:6, :] = records[:6, :]
    for p in range(PRIMS):
        weight = jnp.exp2(jnp.log2(coefficients[p] * scale) * (1.0 / 3.0))
        fields[6 + p : 7 + p, :] = weight * jnp.sqrt(roots[p])
    for move in moves:
        move.wait()


def list_live(pattern, row, order):
    for k in range(NB):
        order[k] = 0

    def step(k, count):
        @pl.when(pattern[row, k] != 0)
        def _():
            order[count] = k

        return count + (pattern[row, k] != 0).astype(jnp.int32)

    return lax.fori_loop(0, NB, step, jnp.int32(0))


def compact_kernel(place, pattern, slices, copies, order, line):
    row = place[0]
    core = row % 2
    count = list_live(pattern, row, order)
    for i in range(line.shape[0]):
        kept = (i < count).astype(jnp.float32)
        line[i] = kept * slices[order[i] // 2, core ^ (order[i] % 2)]
    for copy in range(16):
        copies[copy] = line[...]


def prepare_kernel(place, pattern, iterate_col, high, low):
    col = place[1]
    first = pl.program_id(0) * (PANEL // BLOCK)
    for block in range(PANEL // BLOCK):
        rows = slice(block * BLOCK, (block + 1) * BLOCK)
        for half in range(2):
            lanes = slice(half * BLOCK, (half + 1) * BLOCK)
            mask = live(pattern, first + block, 2 * col + half)
            high[rows, lanes], low[rows, lanes] = split(mask * iterate_col[rows, lanes])


def contract(pieces, high, low):
    total = jnp.zeros((BLOCK, 2 * BLOCK), jnp.float32)
    for k, piece in enumerate(pieces):
        rows = slice(2 * BLOCK * k, 2 * BLOCK * (k + 1))
        piece_high, piece_low = split(piece)
        total = total + jnp.dot(piece_high, high[rows], preferred_element_type=jnp.float32)
        total = total + jnp.dot(piece_high, low[rows], preferred_element_type=jnp.float32)
        total = total + jnp.dot(piece_low, high[rows], preferred_element_type=jnp.float32)
    return total


def live(pattern, row, column):
    return (pattern[row, column] != 0).astype(jnp.float32)


def second_kernel(place, pattern, one_row, high, low, kept, given, total, tile):
    row, col = place[0], place[1]
    part = pl.program_id(0)
    pieces = PART // (2 * BLOCK)
    product = contract([one_row[k] for k in range(pieces)], high, low)

    @pl.when(part == 0)
    def _():
        total[...] = product

    @pl.when(part > 0)
    def _():
        total[...] += product

    @pl.when(part == pl.num_programs(0) - 1)
    def _():
        for half in range(2):
            own = total[:, half * BLOCK : (half + 1) * BLOCK]
            tile[half] = (live(pattern, row, 2 * col + half) * own).T
        core = row % 2
        kept[...] = tile[core].reshape(BLOCK // 8, 8, BLOCK)
        given[...] = tile[1 - core].reshape(BLOCK // 8, 8, BLOCK)


def third_kernel(place, pattern, two_row, high, low, iterate, updated, order):
    row, col = place[0], place[1]
    list_live(pattern, row, order)
    total = jnp.zeros((BLOCK, 2 * BLOCK), jnp.float32)
    for i in range(0, two_row.shape[1], 2):
        pair = [two_row[:, i + h].reshape(BLOCK, BLOCK) for h in range(2)]
        rows = [pl.ds(pl.multiple_of(order[i + h] * BLOCK, BLOCK), BLOCK) for h in range(2)]
        piece_high, piece_low = split(jnp.concatenate(pair, axis=1))
        part_high = jnp.concatenate([high[r, :] for r in rows], axis=0)
        part_low = jnp.concatenate([low[r, :] for r in rows], axis=0)
        total = total + jnp.dot(piece_high, part_high, preferred_element_type=jnp.float32)
        total = total + jnp.dot(piece_high, part_low, preferred_element_type=jnp.float32)
        total = total + jnp.dot(piece_low, part_high, preferred_element_type=jnp.float32)
    for half in range(2):
        lanes = slice(half * BLOCK, (half + 1) * BLOCK)
        mask = live(pattern, row, 2 * col + half)
        updated[:, lanes] = mask * (1.5 * iterate[:, lanes] - 0.5 * total[:, lanes])


def exchange(pieces, axis):
    return lax.all_to_all(pieces, axis, 0, 0, tiled=True)


def call(kernel, out_shapes, scratch, *operands, on_chip=(), outs=None, scalars=2, grid=(), blocks=None, stay=()):
    whole = pl.BlockSpec(memory_space=VMEM)
    in_specs = [pl.BlockSpec(memory_space=SMEM)] * scalars + [whole] * (len(operands) - scalars)
    blocks = blocks or {}
    for k, block in blocks.items():
        if k < len(operands):
            in_specs[k] = pl.BlockSpec(block, lambda i, rest=len(block) - 1: (i,) + (0,) * rest)
    operands = list(operands)
    for k in on_chip:
        operands[k] = pltpu.with_memory_space_constraint(operands[k], VMEM)
    for k in stay:
        operands[k] = pltpu.with_memory_space_constraint(operands[k], HBM)
    if outs is None:
        out_specs = jax.tree.map(lambda _: whole, out_shapes)
    else:
        out_specs = tuple(
            pl.BlockSpec(space, lambda i: (i, 0)) if isinstance(space, tuple) else pl.BlockSpec(memory_space=space)
            for space in outs
        )
        out_specs = out_specs if isinstance(out_shapes, tuple) else out_specs[0]
    return pl.pallas_call(
        kernel,
        out_shape=out_shapes,
        grid=grid,
        in_specs=in_specs,
        out_specs=out_specs,
        scratch_shapes=scratch,
        compiler_params=pltpu.CompilerParams(vmem_limit_bytes=24 * 2**20),
    )(*operands)


def stages(records, pattern, iterate):
    place = jnp.stack([lax.axis_index("row"), lax.axis_index("col")]).astype(jnp.int32)
    fullest = jnp.max(jnp.sum((pattern != 0).astype(jnp.int32), axis=1))
    choice = sum((fullest > room).astype(jnp.int32) for room in ROOMS[:-1])
    place, choice = lax.optimization_barrier((place, choice))
    tile = jax.ShapeDtypeStruct((BLOCK, 2 * BLOCK), jnp.float32)
    stored = HBM((NB * BLOCK, 2 * BLOCK), jnp.bfloat16)
    tiles = HBM((16, BLOCK, 2 * BLOCK), jnp.float32)
    iterate_col = lax.all_gather(iterate, "row", axis=0, tiled=True)
    cores = [[2 * z + core for z in range(16)] for core in range(2)]
    partner = [(r, r ^ 1) for r in range(NB)]
    left = VMEM((2, FIELDS, BLOCK, BLOCK), jnp.float32)
    square = VMEM((BLOCK, BLOCK), jnp.float32)
    table = VMEM((FIELDS, BLOCK), jnp.float32)
    sems = pltpu.SemaphoreType.DMA((16,))
    wide = VMEM((2 * BLOCK, NB * BLOCK), jnp.bfloat16)
    own, copies = call(start_kernel, (table, tiles), [sems], records, iterate, outs=(VMEM, HBM), scalars=0)
    both = jnp.stack([own, lax.ppermute(own, "row", partner)])
    fields = lax.all_gather(both, "row", axis=0, axis_index_groups=cores)
    iterate_row = exchange(copies, "col")
    product_one = call(
        first_kernel,
        tiles,
        [left, square, wide, wide, VMEM((BLOCK, 2 * BLOCK), jnp.float32), sems],
        place,
        pattern,
        fields,
        iterate_row,
        on_chip=(2, 3),
        outs=(HBM,),
    )
    margin = call(margin_kernel, tile, [left, square], place, pattern, fields, on_chip=(2,))
    one_row = exchange(product_one, "col")
    window = (PANEL, 2 * BLOCK)
    high, low = call(
        prepare_kernel,
        (stored, stored),
        [],
        place,
        pattern,
        iterate_col,
        outs=(window, window),
        grid=(NB * BLOCK // PANEL,),
        blocks={2: window},
        stay=(2,),
    )
    half = VMEM((16, 8, BLOCK), jnp.float32)
    turned = VMEM((2, BLOCK, BLOCK), jnp.float32)
    window = (PART, 2 * BLOCK)
    kept, given = call(
        second_kernel,
        (half, half),
        [VMEM((BLOCK, 2 * BLOCK), jnp.float32), turned],
        place,
        pattern,
        one_row,
        high,
        low,
        grid=(NB * BLOCK // PART,),
        blocks={2: (PART // (2 * BLOCK), BLOCK, 2 * BLOCK), 3: window, 4: window},
        stay=(2, 3, 4),
    )
    given = lax.ppermute(given, "row", partner)
    slices = jnp.stack([kept, given], axis=1)
    slices = exchange(slices, "col")
    slices = lax.all_to_all(slices, "row", 0, 0, tiled=True, axis_index_groups=cores)
    order = SMEM((NB,), jnp.int32)

    def finish(room):
        def branch(place, pattern, slices, high, low, iterate):
            line = VMEM((room, 8, BLOCK), jnp.float32)
            copies = VMEM((16, room, 8, BLOCK), jnp.float32)
            copies = call(compact_kernel, copies, [order, line], place, pattern, slices, on_chip=(2,))
            two_row = exchange(copies, "col")
            return call(
                third_kernel, tile, [order], place, pattern, two_row, high, low, iterate, on_chip=(2, 3, 4)
            )

        return branch

    slices, choice = lax.optimization_barrier((slices, choice))
    branches = [finish(room) for room in ROOMS]
    updated = lax.switch(choice, branches, place, pattern, slices, high, low, iterate)
    return (margin, updated)


def solution(mesh):
    in_specs = (P(None, "row"), P(), P("row", "col"))
    out_specs = (P("row", "col"), P("row", "col"))
    return jax.shard_map(stages, mesh=mesh, in_specs=in_specs, out_specs=out_specs, check_vma=False)
```

```python
import jax
import jax.numpy as jnp
from jax import lax
from jax.experimental import pallas as pl
from jax.experimental.pallas import tpu as pltpu
from jax.sharding import PartitionSpec as P


BLOCK = 128
PRIMS = 3
NB = 32
FIELDS = 3 + 2 * PRIMS
CHUNK = 128
PANEL = 1024
PART = 1024
ROOMS = (20, 24, 28, NB)
LOG2E = 1.4426950408889634
VMEM = pltpu.VMEM
SMEM = pltpu.SMEM
HBM = pltpu.HBM


def split(value):
    high = value.astype(jnp.bfloat16)
    low = (value - high.astype(jnp.float32)).astype(jnp.bfloat16)
    return high, low


def dot_transposed(left, right):
    return lax.dot_general(left, right, (((1,), (1,)), ((), ())), preferred_element_type=jnp.float32)


def half_tile(fields_ref, left_ref, tile_ref, half, core, block):
    right = [row_of(fields_ref, core, block, f) for f in range(FIELDS)]

    def chunk(step, carry):
        rows = pl.ds(pl.multiple_of(step * CHUNK, CHUNK), CHUNK)
        left = [left_ref[half, f, rows, :] for f in range(FIELDS)]
        distance = (left[0] - right[0]) ** 2
        distance = distance + (left[1] - right[1]) ** 2
        distance = (distance + (left[2] - right[2]) ** 2) * -LOG2E
        total = jnp.zeros_like(distance)
        for p in range(PRIMS):
            stretched = left[3 + p] * distance
            for q in range(PRIMS):
                inverse_root = lax.rsqrt(left[3 + p] + right[3 + q])
                root = (left[6 + p] * inverse_root) * right[6 + q]
                decay = jnp.exp2((stretched * (inverse_root * inverse_root)) * right[3 + q])
                total = total + ((root * root) * root) * decay
        tile_ref[rows, :] = total
        return carry

    lax.fori_loop(0, BLOCK // CHUNK, chunk, 0)


def row_of(fields, core, block, f):
    return fields[block // 2, core ^ (block % 2), f : f + 1, :]


def spread_own(fields, left, core, col):
    for half in range(2):
        for f in range(FIELDS):
            own = row_of(fields, core, 2 * col + half, f)
            left[half, f] = jnp.broadcast_to(own, (BLOCK, BLOCK)).T


def send_copies(tile, copies, sems):
    moves = [pltpu.make_async_copy(tile, copies.at[k], sems.at[k]) for k in range(16)]
    for move in moves:
        move.start()
    for move in moves:
        move.wait()


def first_kernel(place, pattern, fields, iterate_row, copies, left, tile, high, low, one, sems):
    row, col = place[0], place[1]
    core = row % 2
    spread_own(fields, left, core, col)

    def step(index, carry):
        half, block = index // NB, index % NB
        own = 2 * col + half
        needed = pattern[own, block] * pattern[block, row] * pattern[row, own]
        rows = pl.ds(pl.multiple_of(block * BLOCK, BLOCK), BLOCK)
        lanes = pl.ds(pl.multiple_of(half * BLOCK, BLOCK), BLOCK)

        @pl.when(needed != 0)
        def _():
            half_tile(fields, left, tile, half, core, block)
            high[lanes, rows], low[lanes, rows] = split(tile[...])

        @pl.when(needed == 0)
        def _():
            high[lanes, rows] = jnp.zeros((BLOCK, BLOCK), jnp.bfloat16)
            low[lanes, rows] = jnp.zeros((BLOCK, BLOCK), jnp.bfloat16)

        return carry

    lax.fori_loop(0, 2 * NB, step, 0)
    total = jnp.zeros((BLOCK, 2 * BLOCK), jnp.float32)
    for k in range(16):
        columns = slice(2 * BLOCK * k, 2 * BLOCK * (k + 1))
        piece_high, piece_low = split(iterate_row[k])
        total = total + dot_transposed(piece_high, high[:, columns])
        total = total + dot_transposed(piece_high, low[:, columns])
        total = total + dot_transposed(piece_low, high[:, columns])
    one[...] = total
    send_copies(one, copies, sems)


def margin_kernel(place, pattern, fields, margin, left, tile):
    row, col = place[0], place[1]
    spread_own(fields, left, row % 2, col)
    for half in range(2):
        margin_live = pattern[row, 2 * col + half] != 0
        lanes = slice(half * BLOCK, (half + 1) * BLOCK)

        @pl.when(margin_live)
        def _():
            half_tile(fields, left, tile, half, row % 2, row)
            margin[:, lanes] = tile[...].T

        @pl.when(jnp.logical_not(margin_live))
        def _():
            margin[:, lanes] = jnp.zeros((BLOCK, BLOCK), jnp.float32)


def start_kernel(records, value, fields, copies, sems):
    moves = [pltpu.make_async_copy(value, copies.at[k], sems.at[k]) for k in range(16)]
    for move in moves:
        move.start()
    exponents = [records[3 + p : 4 + p, :] for p in range(PRIMS)]
    coefficients = [records[3 + PRIMS + p : 4 + PRIMS + p, :] for p in range(PRIMS)]
    roots = [jnp.sqrt(e) for e in exponents]
    norm = jnp.zeros_like(exponents[0])
    for p in range(PRIMS):
        for q in range(PRIMS):
            ratio = 2.0 * roots[p] * roots[q] / (exponents[p] + exponents[q])
            norm = norm + coefficients[p] * coefficients[q] * (ratio * jnp.sqrt(ratio))
    scale = (2.0**0.75) * lax.rsqrt(norm)
    fields[:6, :] = records[:6, :]
    for p in range(PRIMS):
        weight = jnp.exp2(jnp.log2(coefficients[p] * scale) * (1.0 / 3.0))
        fields[6 + p : 7 + p, :] = weight * jnp.sqrt(roots[p])
    for move in moves:
        move.wait()


def list_live(pattern, row, order):
    for k in range(NB):
        order[k] = 0

    def step(k, count):
        @pl.when(pattern[row, k] != 0)
        def _():
            order[count] = k

        return count + (pattern[row, k] != 0).astype(jnp.int32)

    return lax.fori_loop(0, NB, step, jnp.int32(0))


def compact_kernel(place, pattern, slices, copies, order, line):
    row = place[0]
    core = row % 2
    count = list_live(pattern, row, order)
    for i in range(line.shape[0]):
        kept = (i < count).astype(jnp.float32)
        line[i] = kept * slices[order[i] // 2, core ^ (order[i] % 2)]
    for copy in range(16):
        copies[copy] = line[...]


def prepare_kernel(place, pattern, iterate_col, high, low):
    col = place[1]
    first = pl.program_id(0) * (PANEL // BLOCK)
    for block in range(PANEL // BLOCK):
        rows = slice(block * BLOCK, (block + 1) * BLOCK)
        for half in range(2):
            lanes = slice(half * BLOCK, (half + 1) * BLOCK)
            mask = live(pattern, first + block, 2 * col + half)
            high[rows, lanes], low[rows, lanes] = split(mask * iterate_col[rows, lanes])


def contract(pieces, high, low):
    total = jnp.zeros((BLOCK, 2 * BLOCK), jnp.float32)
    for k, piece in enumerate(pieces):
        rows = slice(2 * BLOCK * k, 2 * BLOCK * (k + 1))
        piece_high, piece_low = split(piece)
        total = total + jnp.dot(piece_high, high[rows], preferred_element_type=jnp.float32)
        total = total + jnp.dot(piece_high, low[rows], preferred_element_type=jnp.float32)
        total = total + jnp.dot(piece_low, high[rows], preferred_element_type=jnp.float32)
    return total


def live(pattern, row, column):
    return (pattern[row, column] != 0).astype(jnp.float32)


def second_kernel(place, pattern, one_row, high, low, kept, given, total, tile):
    row, col = place[0], place[1]
    part = pl.program_id(0)
    pieces = PART // (2 * BLOCK)
    product = contract([one_row[k] for k in range(pieces)], high, low)

    @pl.when(part == 0)
    def _():
        total[...] = product

    @pl.when(part > 0)
    def _():
        total[...] += product

    @pl.when(part == pl.num_programs(0) - 1)
    def _():
        for half in range(2):
            own = total[:, half * BLOCK : (half + 1) * BLOCK]
            tile[half] = (live(pattern, row, 2 * col + half) * own).T
        core = row % 2
        kept[...] = tile[core].reshape(BLOCK // 8, 8, BLOCK)
        given[...] = tile[1 - core].reshape(BLOCK // 8, 8, BLOCK)


def third_kernel(place, pattern, two_row, high, low, iterate, updated, order):
    row, col = place[0], place[1]
    list_live(pattern, row, order)
    total = jnp.zeros((BLOCK, 2 * BLOCK), jnp.float32)
    for i in range(0, two_row.shape[1], 2):
        pair = [two_row[:, i + h].reshape(BLOCK, BLOCK) for h in range(2)]
        rows = [pl.ds(pl.multiple_of(order[i + h] * BLOCK, BLOCK), BLOCK) for h in range(2)]
        piece_high, piece_low = split(jnp.concatenate(pair, axis=1))
        part_high = jnp.concatenate([high[r, :] for r in rows], axis=0)
        part_low = jnp.concatenate([low[r, :] for r in rows], axis=0)
        total = total + jnp.dot(piece_high, part_high, preferred_element_type=jnp.float32)
        total = total + jnp.dot(piece_high, part_low, preferred_element_type=jnp.float32)
        total = total + jnp.dot(piece_low, part_high, preferred_element_type=jnp.float32)
    for half in range(2):
        lanes = slice(half * BLOCK, (half + 1) * BLOCK)
        mask = live(pattern, row, 2 * col + half)
        updated[:, lanes] = mask * (1.5 * iterate[:, lanes] - 0.5 * total[:, lanes])


def exchange(pieces, axis):
    return lax.all_to_all(pieces, axis, 0, 0, tiled=True)


def call(kernel, out_shapes, scratch, *operands, on_chip=(), outs=None, scalars=2, grid=(), blocks=None, stay=()):
    whole = pl.BlockSpec(memory_space=VMEM)
    in_specs = [pl.BlockSpec(memory_space=SMEM)] * scalars + [whole] * (len(operands) - scalars)
    blocks = blocks or {}
    for k, block in blocks.items():
        if k < len(operands):
            in_specs[k] = pl.BlockSpec(block, lambda i, rest=len(block) - 1: (i,) + (0,) * rest)
    operands = list(operands)
    for k in on_chip:
        operands[k] = pltpu.with_memory_space_constraint(operands[k], VMEM)
    for k in stay:
        operands[k] = pltpu.with_memory_space_constraint(operands[k], HBM)
    if outs is None:
        out_specs = jax.tree.map(lambda _: whole, out_shapes)
    else:
        out_specs = tuple(
            pl.BlockSpec(space, lambda i: (i, 0)) if isinstance(space, tuple) else pl.BlockSpec(memory_space=space)
            for space in outs
        )
        out_specs = out_specs if isinstance(out_shapes, tuple) else out_specs[0]
    return pl.pallas_call(
        kernel,
        out_shape=out_shapes,
        grid=grid,
        in_specs=in_specs,
        out_specs=out_specs,
        scratch_shapes=scratch,
        compiler_params=pltpu.CompilerParams(vmem_limit_bytes=24 * 2**20),
    )(*operands)


def stages(records, pattern, iterate):
    place = jnp.stack([lax.axis_index("row"), lax.axis_index("col")]).astype(jnp.int32)
    tile = jax.ShapeDtypeStruct((BLOCK, 2 * BLOCK), jnp.float32)
    stored = HBM((NB * BLOCK, 2 * BLOCK), jnp.bfloat16)
    tiles = HBM((16, BLOCK, 2 * BLOCK), jnp.float32)
    iterate_col = lax.all_gather(iterate, "row", axis=0, tiled=True)
    cores = [[2 * z + core for z in range(16)] for core in range(2)]
    partner = [(r, r ^ 1) for r in range(NB)]
    left = VMEM((2, FIELDS, BLOCK, BLOCK), jnp.float32)
    square = VMEM((BLOCK, BLOCK), jnp.float32)
    table = VMEM((FIELDS, BLOCK), jnp.float32)
    sems = pltpu.SemaphoreType.DMA((16,))
    wide = VMEM((2 * BLOCK, NB * BLOCK), jnp.bfloat16)
    own, copies = call(start_kernel, (table, tiles), [sems], records, iterate, outs=(VMEM, HBM), scalars=0)
    both = jnp.stack([own, lax.ppermute(own, "row", partner)])
    fields = lax.all_gather(both, "row", axis=0, axis_index_groups=cores)
    iterate_row = exchange(copies, "col")
    product_one = call(
        first_kernel,
        tiles,
        [left, square, wide, wide, VMEM((BLOCK, 2 * BLOCK), jnp.float32), sems],
        place,
        pattern,
        fields,
        iterate_row,
        on_chip=(2, 3),
        outs=(HBM,),
    )
    margin = call(margin_kernel, tile, [left, square], place, pattern, fields, on_chip=(2,))
    product_one, late = lax.optimization_barrier((product_one, pattern))
    fullest = jnp.max(jnp.sum((late != 0).astype(jnp.int32), axis=1))
    choice = sum((fullest > room).astype(jnp.int32) for room in ROOMS[:-1])
    one_row = exchange(product_one, "col")
    window = (PANEL, 2 * BLOCK)
    high, low = call(
        prepare_kernel,
        (stored, stored),
        [],
        place,
        pattern,
        iterate_col,
        outs=(window, window),
        grid=(NB * BLOCK // PANEL,),
        blocks={2: window},
        stay=(2,),
    )
    high, choice = lax.optimization_barrier((high, choice))
    half = VMEM((16, 8, BLOCK), jnp.float32)
    turned = VMEM((2, BLOCK, BLOCK), jnp.float32)
    window = (PART, 2 * BLOCK)
    kept, given = call(
        second_kernel,
        (half, half),
        [VMEM((BLOCK, 2 * BLOCK), jnp.float32), turned],
        place,
        pattern,
        one_row,
        high,
        low,
        grid=(NB * BLOCK // PART,),
        blocks={2: (PART // (2 * BLOCK), BLOCK, 2 * BLOCK), 3: window, 4: window},
        stay=(2, 3, 4),
    )
    given = lax.ppermute(given, "row", partner)
    slices = jnp.stack([kept, given], axis=1)
    slices = exchange(slices, "col")
    slices = lax.all_to_all(slices, "row", 0, 0, tiled=True, axis_index_groups=cores)
    order = SMEM((NB,), jnp.int32)

    def finish(room):
        def branch(place, pattern, slices, high, low, iterate):
            line = VMEM((room, 8, BLOCK), jnp.float32)
            copies = VMEM((16, room, 8, BLOCK), jnp.float32)
            copies = call(compact_kernel, copies, [order, line], place, pattern, slices, on_chip=(2,))
            two_row = exchange(copies, "col")
            return call(
                third_kernel, HBM((BLOCK, 2 * BLOCK), jnp.float32), [order], place, pattern, two_row, high, low, iterate, on_chip=(2, 3, 4)
            )

        return branch

    slices, choice = lax.optimization_barrier((slices, choice))
    branches = [finish(room) for room in ROOMS]
    updated = lax.switch(choice, branches, place, pattern, slices, high, low, iterate)
    return (margin, updated)


def solution(mesh):
    in_specs = (P(None, "row"), P(), P("row", "col"))
    out_specs = (P("row", "col"), P("row", "col"))
    return jax.shard_map(stages, mesh=mesh, in_specs=in_specs, out_specs=out_specs, check_vma=False)
```
